32 devices in a mesh: seq: 8 (over z, x), head: 4 (over y, core).
Axes of the slice: x: 2, y: 2, z: 4, core: 2. Of those that a mesh axis runs over, the one named last changes fastest.
Arguments:
- queries: bfloat16 [1024, 6144], P('seq', 'head'), may hold values from -6 to 6
- keys: bfloat16 [1024, 6144], P('seq', 'head'), may hold values from -6 to 6
- values: bfloat16 [1024, 6144], P('seq', 'head'), may hold values from -6 to 6
- log_decay: float32 [1024, 48], P('seq', 'head'), may hold values from -1 to 0, as said below
- out_gate: bfloat16 [1024, 6144], P('seq', 'head'), may hold values from -6 to 6
- attn_gain: bfloat16 [6144], P('head'), may hold values from 0.5 to 1.5
- residual: bfloat16 [1024, 6144], P('seq', 'head'), may hold values from -6 to 6
- moe_gain: bfloat16 [6144], P('head'), may hold values from 0.5 to 1.5
- router: bfloat16 [6144, 8], P('head'), may hold values from -0.078125 to 0.078125
- routes: int32 [1024, 2], P('seq'), may hold values from 0 to 7, all different within a row; in each aligned block of 128 rows (0 to 127, 128 to 255, ...) at most 36 rows name the same one
- w_gate: bfloat16 [6144, 36864], P('head', 'seq'), may hold values from -0.078125 to 0.078125
- w_up: bfloat16 [6144, 36864], P('head', 'seq'), may hold values from -0.078125 to 0.078125
- w_down: bfloat16 [36864, 6144], P('seq', 'head'), may hold values from -0.09375 to 0.09375
Outputs:
- layer_out: bfloat16 [1024, 6144], P('seq', 'head')
The draws below stay inside these ranges and needn't reach their ends.
Inputs may be any that keep to these rules, and one draw needn't show every extreme that they name: `routes`: each row names two different experts; in the rows of one device (aligned blocks of 128 rows) no expert is named by more than 36 rows, a bound that some block reaches. `log_decay`: every entry is negative.
All inputs are finite; a program needn't handle non-finite values.
Results may differ from the reference program's by a relative error of at most 0.0055.
Values may be sent and summed in bfloat16 or wider, within the bound.
No kernel may reach another device: no remote copies, remote signals or barrier semaphores. Data moves between devices by JAX's collectives and lax.ppermute only.
A program may use at most 128 MiB of HBM per device.

```python
import math
import jax
import jax.numpy as jnp
import numpy as np
from jax import lax

D = 6144
HEADS = 48
HD = 128
FFE = 4608
EXPERTS = 8
TOK_DEV = 128
TOKEN_TOTAL = 1024
OWNERS = 1
CAP = 36
N_SEQ = 8


def draw_log_decay(key, part):
    random_subkeys = jax.random.split(key, 6)
    fast_share = 0.5
    chooser = jax.random.uniform(random_subkeys[0], (1, HEADS))
    fast_rate = jnp.exp(jax.random.uniform(random_subkeys[1], (1, HEADS), minval=math.log(1.0 / 50.0), maxval=math.log(1.0 / 30.0)))
    slow_rate = jnp.exp(jax.random.uniform(random_subkeys[2], (1, HEADS), minval=math.log(0.05), maxval=math.log(0.5))) / TOKEN_TOTAL
    baseline_decay_rate = jnp.where(chooser < fast_share, fast_rate, slow_rate)
    jaggedness = jnp.exp(jax.random.uniform(random_subkeys[3], (TOKEN_TOTAL, HEADS), minval=-0.6931, maxval=0.6931))
    spike_strike = jax.random.uniform(random_subkeys[4], (TOKEN_TOTAL, 1)) < 2.0 / TOKEN_TOTAL
    spike_magnitude = jnp.log(jax.random.uniform(random_subkeys[5], (TOKEN_TOTAL, 1), minval=0.5, maxval=0.8))
    return (-baseline_decay_rate * jaggedness + jnp.where(spike_strike, spike_magnitude, 0.0)).astype(jnp.float32)


def levels(stream_key, shape, shards, low, high):
    def one(position, shards_of):
        steps = jax.random.uniform(jax.random.fold_in(jax.random.fold_in(stream_key, 6), position), (shards_of,), jnp.float32, low / len(shards), high / len(shards))
        return jnp.repeat(jnp.exp(steps), shape[position] // shards_of).reshape((-1,) + (1,) * (len(shape) - position - 1))

    factor_of = one(*shards[0])
    for cut in shards[1:]:
        factor_of = factor_of * one(*cut)
    return factor_of


def deal_out(key, own, number, rows, amount, top, limit, lean):
    order = jax.random.permutation(key, amount)
    heavy_load, common = load_shares(amount, rows * top, limit, lean, True), load_shares(amount, rows * top, limit, lean, False)
    places = jnp.arange(amount)

    def named(sizes, turn):
        used = int((sizes > 0).sum())
        fixed = max(1, used // 4)
        passed = fixed + (places - fixed + turn * (used - fixed)) % max(1, amount - fixed)
        return jnp.zeros((amount,), jnp.int32).at[order[jnp.where(places < fixed, places, passed)]].set(jnp.asarray(sizes, jnp.int32))

    sizes = jnp.where(number % 4 == 0, named(heavy_load, number // 4), named(common, number - number // 4 - 1))
    mixed = jax.random.permutation(jax.random.fold_in(own, 3), amount)
    source_of, receiver = mixed[0:amount // 2 * 2:2], mixed[1:amount // 2 * 2:2]
    room = jnp.minimum(sizes[source_of] - 1, limit - sizes[receiver]) // 2
    room = jnp.where((source_of == order[0]) | (receiver == order[0]) | (sizes[receiver] == 0), 0, jnp.maximum(room, 0))
    passed = jax.random.randint(jax.random.fold_in(own, 4), (amount // 2,), 0, 1 << 20) % (room + 1)
    sizes = sizes.at[source_of].add(-passed).at[receiver].add(passed)
    members = jnp.searchsorted(jnp.cumsum(sizes), jnp.arange(rows * top), side="right").astype(jnp.int32)
    listing = members.reshape(top, rows).T
    listing = listing[jax.random.permutation(jax.random.fold_in(own, 1), rows)]
    turn = jax.random.randint(jax.random.fold_in(own, 2), (rows, 1), 0, top)
    return jnp.take_along_axis(listing, (jnp.arange(top)[None, :] + turn) % top, axis=1)


def load_shares(number_of, total, limit, lean, full):
    loads = [(1 << 20) // math.isqrt(standing ** lean) + 1 for standing in range(1, number_of + 1)]
    largest = limit if full else min(limit, max(-(-total // number_of), total * loads[0] // sum(loads)))
    least = 1 if total - largest >= number_of - 1 else 0
    given, surplus = [largest] + [least] * (number_of - 1), total - largest - least * (number_of - 1)
    while surplus > 0:
        movable = [i for i in range(1, number_of) if given[i] < largest] or [i for i in range(1, number_of) if given[i] < limit]
        mass, left = sum([loads[i] for i in movable]), surplus
        for i in movable:
            extra = min(limit - given[i], max(1, left * loads[i] // mass), surplus)
            given[i] = given[i] + extra
            surplus = surplus - extra
    return np.array(given)


def noise(own_key, dims, width, limit, cuts=(), kind=jnp.bfloat16):
    loudness = levels(own_key, dims, cuts, -0.22, 0.18) if cuts else 1.0
    entries = jax.random.normal(own_key, dims, jnp.float32) * width * loudness
    return jnp.minimum(jnp.maximum(entries, -limit), limit).astype(kind)


def setup_inputs(seed: int = 0) -> dict:
    key_list = jax.random.split(jax.random.key(seed), 14)
    queries = noise(key_list[0], (TOKEN_TOTAL, D), 1.0, 6.0, ((0, 8), (1, 4)))
    keys = noise(key_list[1], (TOKEN_TOTAL, D), 1.0, 6.0, ((0, 8), (1, 4)))
    values = noise(key_list[2], (TOKEN_TOTAL, D), 1.0, 6.0, ((0, 8), (1, 4)))
    log_decay = draw_log_decay(jax.random.fold_in(key_list[13], 71), 0)
    out_gate = noise(key_list[4], (TOKEN_TOTAL, D), 1.0, 6.0, ((0, 8), (1, 4)))
    attn_gain = jnp.clip(1.0 + 0.1 * jax.random.normal(key_list[5], (D,), jnp.float32), 0.5, 1.5).astype(jnp.bfloat16)
    residual = noise(key_list[6], (TOKEN_TOTAL, D), 1.0, 6.0, ((0, 8), (1, 4)))
    moe_gain = jnp.clip(1.0 + 0.1 * jax.random.normal(key_list[7], (D,), jnp.float32), 0.5, 1.5).astype(jnp.bfloat16)
    router = noise(key_list[8], (D, EXPERTS), D ** -0.5, 0.078125, ((0, 4),))
    routes_keys = jax.random.split(jax.random.fold_in(key_list[9], 1), TOKEN_TOTAL // TOK_DEV)
    routes_turns = jax.random.permutation(jax.random.fold_in(key_list[9], 3), TOKEN_TOTAL // TOK_DEV)
    routes = jax.vmap(lambda own, number: deal_out(jax.random.fold_in(key_list[9], 2), own, number, TOK_DEV, EXPERTS, 2, CAP, 2))(routes_keys, routes_turns).reshape((TOKEN_TOTAL, 2))
    w_gate = noise(key_list[10], (D, EXPERTS * FFE), D ** -0.5, 0.078125, ((0, 4), (1, 8)))
    w_up = noise(key_list[11], (D, EXPERTS * FFE), D ** -0.5, 0.078125, ((0, 4), (1, 8)))
    w_down = noise(key_list[12], (EXPERTS * FFE, D), FFE ** -0.5, 0.09375, ((0, 8), (1, 4)))
    return dict(queries=queries, keys=keys, values=values, log_decay=log_decay, out_gate=out_gate, attn_gain=attn_gain, residual=residual, moe_gain=moe_gain, router=router, routes=routes, w_gate=w_gate, w_up=w_up, w_down=w_down)


def block_terms(query_act, key_act, value_all, decay_log):
    length = query_act.shape[0]
    cumulative = jnp.cumsum(decay_log, axis=0)
    row_index = lax.broadcasted_iota(jnp.int32, (length, length), 0)
    col_index = lax.broadcasted_iota(jnp.int32, (length, length), 1)
    causal = (row_index >= col_index)[None, :, :]
    by_head = jnp.transpose(cumulative)
    spread = by_head[:, :, None] - by_head[:, None, :]
    weight = jnp.where(causal, jnp.exp(jnp.where(causal, spread, 0.0)), 0.0)
    scores = jnp.einsum('ihe,jhe->hij', query_act, key_act, precision=lax.Precision.HIGHEST) * weight
    inner_part = jnp.einsum('hij,jhe->ihe', scores, value_all, precision=lax.Precision.HIGHEST)
    tail_decay = jnp.exp(cumulative[-1][None, :] - cumulative)
    local_state = jnp.einsum('jhe,jhf->hef', key_act * tail_decay[:, :, None], value_all, precision=lax.Precision.HIGHEST)
    return (cumulative, inner_part, local_state, jnp.exp(cumulative[-1]))

def attention_out(inner_part, cumulative, carry_state, query_act):
    earlier = jnp.einsum('ihe,hef->ihf', query_act, carry_state, precision=lax.Precision.HIGHEST)
    return inner_part + jnp.exp(cumulative)[:, :, None] * earlier

def finish(attn, attn_gain, out_gate, residual):
    mean_sq = lax.optimization_barrier(jnp.mean(attn * attn, axis=-1, keepdims=True))
    normed_heads = attn * lax.rsqrt(mean_sq + 1e-06)
    flat = normed_heads.reshape(attn.shape[0], attn.shape[1] * attn.shape[2])
    gated = flat * attn_gain.astype(jnp.float32) * jax.nn.sigmoid(out_gate.astype(jnp.float32))
    return (residual.astype(jnp.float32) + gated).astype(jnp.bfloat16)

def moe_input(hidden, moe_gain):
    wide = hidden.astype(jnp.float32)
    mean_sq = lax.optimization_barrier(jnp.mean(wide * wide, axis=-1, keepdims=True))
    return (wide * lax.rsqrt(mean_sq + 1e-06) * moe_gain.astype(jnp.float32)).astype(jnp.bfloat16)

def gate_weights(logits, routes):
    expert_ids = lax.broadcasted_iota(jnp.int32, (1, 1, logits.shape[1]), 2)
    onehot = routes[:, :, None] == expert_ids
    picked = lax.optimization_barrier(jnp.sum(jnp.where(onehot, logits[:, None, :], 0.0), axis=-1))
    return jax.nn.sigmoid(picked - picked[:, ::-1])

def slot_table(routes, expert_count, capacity):
    flat_ids = routes.reshape(-1)
    expert_ids = lax.broadcasted_iota(jnp.int32, (1, expert_count), 1)
    onehot = (flat_ids[:, None] == expert_ids).astype(jnp.int32)
    ranking = jnp.cumsum(onehot, axis=0) - onehot
    own_rank = lax.optimization_barrier(jnp.sum(ranking * onehot, axis=1))
    slot_ids = flat_ids * capacity + own_rank
    slot_range = lax.broadcasted_iota(jnp.int32, (1, expert_count * capacity), 1)
    return (slot_ids[:, None] == slot_range).astype(jnp.float32)

def reference(queries, keys, values, log_decay, out_gate, attn_gain, residual, moe_gain, router, routes, w_gate, w_up, w_down):
    query_act = jax.nn.silu(queries.astype(jnp.float32)).reshape(N_SEQ, TOK_DEV, HEADS, HD)
    key_act = jax.nn.silu(keys.astype(jnp.float32)).reshape(N_SEQ, TOK_DEV, HEADS, HD)
    value_all = values.astype(jnp.float32).reshape(N_SEQ, TOK_DEV, HEADS, HD)
    decay_blocks = log_decay.reshape(N_SEQ, TOK_DEV, HEADS)

    def advance(carry_state, block_data):
        query_blk, key_blk, value_blk, decay_blk = block_data
        cumulative, inner_part, local_state, block_decay = block_terms(query_blk, key_blk, value_blk, decay_blk)
        result = attention_out(inner_part, cumulative, carry_state, query_blk)
        return (block_decay[:, None, None] * carry_state + local_state, result)
    initial_state = jnp.zeros((HEADS, HD, HD), jnp.float32)
    unused, attn = lax.scan(advance, initial_state, (query_act, key_act, value_all, decay_blocks))
    attn = attn.reshape(TOKEN_TOTAL, HEADS, HD)
    hidden = finish(attn, attn_gain, out_gate, residual)
    normed = moe_input(hidden, moe_gain)
    logits = jnp.dot(normed, router, preferred_element_type=jnp.float32)
    weights = gate_weights(logits, routes)
    route_blocks = routes.reshape(N_SEQ, TOK_DEV, 2)
    tables = jax.vmap(lambda block_routes: slot_table(block_routes, EXPERTS, CAP))(route_blocks)
    doubled = jnp.repeat(normed.reshape(N_SEQ, TOK_DEV, D), 2, axis=1)
    packed = jnp.einsum('nas,nad->nsd', tables, doubled.astype(jnp.float32), precision=lax.Precision.HIGHEST).astype(jnp.bfloat16)
    packed = packed.reshape(N_SEQ, EXPERTS, CAP, D).transpose(1, 0, 2, 3).reshape(EXPERTS, N_SEQ * CAP, D)
    groups = OWNERS
    share_cols = FFE // groups

    def expert(expert_idx):
        tok_rows = lax.dynamic_index_in_dim(packed, expert_idx, 0, keepdims=False).astype(jnp.float32)
        gate_cols = lax.dynamic_slice_in_dim(w_gate, expert_idx * FFE, FFE, 1).reshape(D, groups, share_cols).astype(jnp.float32)
        up_cols = lax.dynamic_slice_in_dim(w_up, expert_idx * FFE, FFE, 1).reshape(D, groups, share_cols).astype(jnp.float32)
        down_rows = lax.dynamic_slice_in_dim(w_down, expert_idx * FFE, FFE, 0).reshape(groups, share_cols, D).astype(jnp.float32)
        gate = jnp.einsum('rd,dgc->grc', tok_rows, gate_cols)
        upward = jnp.einsum('rd,dgc->grc', tok_rows, up_cols)
        act = (jax.nn.silu(gate) * upward).astype(jnp.bfloat16)
        shares = jnp.einsum('grc,gcd->grd', act.astype(jnp.float32), down_rows).astype(jnp.bfloat16)
        return lax.optimization_barrier(jnp.sum(shares.astype(jnp.float32), axis=0))
    expert_out = lax.map(expert, jnp.arange(EXPERTS, dtype=jnp.int32))
    expert_out = expert_out.reshape(EXPERTS, N_SEQ, CAP, D).transpose(1, 0, 2, 3).reshape(N_SEQ, EXPERTS * CAP, D)
    weighted = tables * weights.reshape(N_SEQ, 2 * TOK_DEV)[:, :, None]
    per_token = weighted.reshape(N_SEQ, TOK_DEV, 2, EXPERTS * CAP).sum(axis=2)
    moe = jnp.einsum('nts,nsd->ntd', per_token, expert_out, precision=lax.Precision.HIGHEST).reshape(TOKEN_TOTAL, D)
    return (hidden.astype(jnp.float32) + moe).astype(jnp.bfloat16)
```

```python
import functools

import jax
import jax.numpy as jnp
from jax import lax
from jax.experimental import pallas as pl
from jax.experimental.pallas import tpu as pltpu
from jax.sharding import PartitionSpec as P


def prefix_2(value, axis, join, neutral):
    count, mine = (lax.axis_size(axis), lax.axis_index(axis))
    pieces = jax.tree.map(lambda part: lax.all_gather(part, axis), value)
    subtotal = jax.tree.map(
        lambda part, zero: jnp.full_like(part, 0) + jnp.asarray(zero, part.dtype), value, neutral
    )

    def lap(position, subtotal):
        longer = join(subtotal, jax.tree.map(lambda part: part[position], pieces))
        return jax.tree.map(lambda new, old: jnp.where(position < mine, new, old), longer, subtotal)

    return lax.fori_loop(0, count - 1, lap, subtotal)


def block_terms(query_act, key_act, value_all, decay_log):
    length = query_act.shape[0]
    cumulative = jnp.cumsum(decay_log, axis=0)
    row_index = lax.broadcasted_iota(jnp.int32, (length, length), 0)
    col_index = lax.broadcasted_iota(jnp.int32, (length, length), 1)
    causal = (row_index >= col_index)[None, :, :]
    by_head = jnp.transpose(cumulative)
    spread = by_head[:, :, None] - by_head[:, None, :]
    weight = jnp.where(causal, jnp.exp(jnp.where(causal, spread, 0.0)), 0.0)
    scores = (
        jnp.einsum("ihe,jhe->hij", query_act, key_act, precision=lax.Precision.HIGHEST) * weight
    )
    inner_part = jnp.einsum("hij,jhe->ihe", scores, value_all, precision=lax.Precision.HIGHEST)
    tail_decay = jnp.exp(cumulative[-1][None, :] - cumulative)
    local_state = jnp.einsum(
        "jhe,jhf->hef", key_act * tail_decay[:, :, None], value_all, precision=lax.Precision.HIGHEST
    )
    return (cumulative, inner_part, local_state, jnp.exp(cumulative[-1]))


def attention_out(inner_part, cumulative, carry_state, query_act):
    earlier = jnp.einsum("ihe,hef->ihf", query_act, carry_state, precision=lax.Precision.HIGHEST)
    return inner_part + jnp.exp(cumulative)[:, :, None] * earlier


def finish(attn, attn_gain, out_gate, residual):
    mean_sq = jnp.mean(attn * attn, axis=-1, keepdims=True)
    normed_heads = attn * lax.rsqrt(mean_sq + 1e-06)
    flat = normed_heads.reshape(attn.shape[0], attn.shape[1] * attn.shape[2])
    gated = flat * attn_gain.astype(jnp.float32) * jax.nn.sigmoid(out_gate.astype(jnp.float32))
    return (residual.astype(jnp.float32) + gated).astype(jnp.bfloat16)


def gate_weights(logits, routes):
    expert_ids = lax.broadcasted_iota(jnp.int32, (1, 1, logits.shape[1]), 2)
    onehot = routes[:, :, None] == expert_ids
    picked = jnp.sum(jnp.where(onehot, logits[:, None, :], 0.0), axis=-1)
    return jax.nn.sigmoid(picked - picked[:, ::-1])


def slot_table(routes, expert_count, capacity):
    flat_ids = routes.reshape(-1)
    expert_ids = lax.broadcasted_iota(jnp.int32, (1, expert_count), 1)
    onehot = (flat_ids[:, None] == expert_ids).astype(jnp.int32)
    ranking = jnp.cumsum(onehot, axis=0) - onehot
    own_rank = jnp.sum(ranking * onehot, axis=1)
    slot_ids = flat_ids * capacity + own_rank
    slot_range = lax.broadcasted_iota(jnp.int32, (1, expert_count * capacity), 1)
    return (slot_ids[:, None] == slot_range).astype(jnp.float32)


def build_sends(tok_rows, slot_bf16, expert_count, capacity, owner_count):
    doubled = jnp.repeat(tok_rows, 2, axis=0)
    packed = jnp.einsum("as,ad->sd", slot_bf16, doubled, preferred_element_type=jnp.float32).astype(
        jnp.bfloat16
    )
    width = tok_rows.shape[1]
    fanned = jnp.broadcast_to(
        packed.reshape(expert_count, 1, capacity, width),
        (expert_count, owner_count, capacity, width),
    )
    return fanned.reshape(expert_count * owner_count, capacity, width)


def local_general(
    queries,
    keys,
    values,
    log_decay,
    out_gate,
    attn_gain,
    residual,
    moe_gain,
    router,
    routes,
    w_gate,
    w_up,
    w_down,
):
    tok_count = queries.shape[0]
    heads_here = log_decay.shape[1]
    head_size = queries.shape[1] // heads_here
    query_act = jax.nn.silu(queries.astype(jnp.float32)).reshape(tok_count, heads_here, head_size)
    key_act = jax.nn.silu(keys.astype(jnp.float32)).reshape(tok_count, heads_here, head_size)
    value_all = values.astype(jnp.float32).reshape(tok_count, heads_here, head_size)
    cumulative, inner_part, local_state, block_decay = block_terms(
        query_act, key_act, value_all, log_decay
    )

    def combine(earlier, later):
        return (earlier[0] * later[0], later[0][:, None, None] * earlier[1] + later[1])

    identity = (jnp.ones_like(block_decay), jnp.zeros_like(local_state))
    prefix = prefix_2((block_decay, local_state), "seq", combine, identity)
    attn = attention_out(inner_part, cumulative, prefix[1], query_act)
    hidden = finish(attn, attn_gain, out_gate, residual)
    part_width = hidden.shape[1]
    full_width = part_width * lax.axis_size("head")
    wide = hidden.astype(jnp.float32)
    squares = lax.psum(jnp.sum(wide * wide, axis=1), "head")
    scale = lax.rsqrt(squares / full_width + 1e-06)
    normed = (wide * scale[:, None] * moe_gain.astype(jnp.float32)).astype(jnp.bfloat16)
    logits = lax.psum(jnp.dot(normed, router, preferred_element_type=jnp.float32), "head")
    weights = gate_weights(logits, routes)
    expert_count = router.shape[1]
    owner_count = lax.axis_size("seq") // expert_count
    capacity = 2 * tok_count // expert_count + max(1, tok_count // 32)
    table = slot_table(routes, expert_count, capacity)
    outgoing = build_sends(normed, table.astype(jnp.bfloat16), expert_count, capacity, owner_count)
    arrived = lax.all_to_all(outgoing, "seq", split_axis=0, concat_axis=0, tiled=True)
    sources, items, width = arrived.shape
    flat_rows = arrived.reshape(sources * items, width)
    gate_part = jnp.dot(flat_rows, w_gate, preferred_element_type=jnp.float32)
    up_part = jnp.dot(flat_rows, w_up, preferred_element_type=jnp.float32)
    gate = lax.psum_scatter(gate_part, "head", scatter_dimension=1, tiled=True)
    upward = lax.psum_scatter(up_part, "head", scatter_dimension=1, tiled=True)
    act = (jax.nn.silu(gate) * upward).astype(jnp.bfloat16)
    act = lax.all_gather(act, "head", axis=1, tiled=True)
    result = jnp.dot(act, w_down, preferred_element_type=jnp.float32).astype(jnp.bfloat16)
    shares = result.reshape(sources, items, width)
    returned = lax.all_to_all(shares, "seq", split_axis=0, concat_axis=0, tiled=True)
    summed = (
        returned.astype(jnp.float32)
        .reshape(expert_count, owner_count, capacity, part_width)
        .sum(axis=1)
    )
    summed = summed.reshape(expert_count * capacity, part_width)
    per_token = (
        (table * weights.reshape(-1)[:, None])
        .reshape(tok_count, 2, expert_count * capacity)
        .sum(axis=1)
    )
    moe = jnp.dot(per_token, summed, precision=lax.Precision.HIGHEST)
    return (hidden.astype(jnp.float32) + moe).astype(jnp.bfloat16)


F32, BF16 = jnp.float32, jnp.bfloat16
LANES = 128
PAD = 16
NT = (((1,), (1,)), ((), ()))
TN = (((0,), (0,)), ((), ()))


def mm(a, b, dims=(((1,), (0,)), ((), ()))):
    return lax.dot_general(a, b, dims, preferred_element_type=F32)


def exact(a, b, dims=(((1,), (0,)), ((), ()))):
    return lax.dot_general(
        a, b, dims, preferred_element_type=F32, precision=lax.Precision.HIGHEST
    )


def split2(a):
    high = a.astype(BF16)
    return high, (a - high.astype(F32)).astype(BF16)


def silu(a):
    return a / (1.0 + jnp.exp(-a))


def decay_rows(decay_ref):
    heads, length = decay_ref.shape
    row = lax.broadcasted_iota(jnp.int32, (length, length), 0)
    col = lax.broadcasted_iota(jnp.int32, (length, length), 1)
    return exact(decay_ref[...], (row <= col).astype(F32)), row, col


def spread(values):
    high, low = split2(jnp.broadcast_to(values, (values.shape[0], LANES)))
    rest = PAD - 2 * values.shape[0]
    return jnp.concatenate([high, low, jnp.zeros((rest, LANES), BF16)], axis=0)


def state_kernel(place_ref, keys_ref, values_ref, decay_ref, sent_ref, kept_ref, own_ref, all_ref, dec_ref):
    heads, length = decay_ref.shape
    half = heads // 2
    cum, _, _ = decay_rows(decay_ref)
    total = cum[:, length - 1 :]
    tail = jnp.transpose(jnp.exp(total - cum))
    whole = jnp.exp(total)
    for h in range(heads):
        lanes = pl.ds(h * LANES, LANES)
        act = silu(keys_ref[:, lanes].astype(F32)) * tail[:, h : h + 1]
        high, low = split2(act)
        value = values_ref[:, lanes]
        all_ref[h] = mm(high, value, TN) + mm(low, value, TN)
    dec_ref[0] = jnp.broadcast_to(whole[:half], (half, LANES))
    dec_ref[1] = jnp.broadcast_to(whole[half:], (half, LANES))
    mine = place_ref[0] % 2
    for i in range(half):
        sent_ref[pl.ds(i * LANES, LANES), :] = all_ref[(1 - mine) * half + i].astype(BF16)
        kept_ref[i] = all_ref[mine * half + i]
    sent_ref[pl.ds(half * LANES, PAD), :] = spread(dec_ref[1 - mine])
    own_ref[...] = dec_ref[mine]


def inner_kernel(
    queries_ref, keys_ref, values_ref, decay_ref, gain_ref, gate_ref, inner_ref, high_ref, low_ref, gate_out_ref
):
    heads, length = decay_ref.shape
    cum, row, col = decay_rows(decay_ref)
    columns = jnp.transpose(cum)
    grown = jnp.exp(columns)
    causal = row >= col
    for h in range(heads):
        lanes = pl.ds(h * LANES, LANES)
        query = silu(queries_ref[:, lanes].astype(F32))
        high_ref[:, lanes], low_ref[:, lanes] = split2(query * grown[:, h : h + 1])
        q_high, q_low = split2(query)
        k_high, k_low = split2(silu(keys_ref[:, lanes].astype(F32)))
        gap = jnp.where(causal, columns[:, h : h + 1] - cum[h : h + 1, :], 0.0)
        weight = jnp.where(causal, jnp.exp(gap), 0.0)
        scores = (mm(q_high, k_high, NT) + (mm(q_high, k_low, NT) + mm(q_low, k_high, NT))) * weight
        high, low = split2(scores)
        value = values_ref[:, lanes]
        inner_ref[:, lanes] = mm(high, value) + mm(low, value)
        gate = 1.0 / (1.0 + jnp.exp(-gate_ref[:, lanes].astype(F32)))
        gate_out_ref[:, lanes] = gate * gain_ref[:, lanes].astype(F32)


def expert_table(routes_ref, count):
    length = routes_ref.shape[1]
    ids = lax.broadcasted_iota(jnp.int32, (count, length), 0)
    first = routes_ref[0:1, :] == ids
    second = routes_ref[1:2, :] == ids
    named = jnp.where(first | second, 1.0, 0.0)
    row = lax.broadcasted_iota(jnp.int32, (length, length), 0)
    col = lax.broadcasted_iota(jnp.int32, (length, length), 1)
    rank = mm(named.astype(BF16), jnp.where(row < col, 1.0, 0.0).astype(BF16))
    return first, second, jnp.where(named > 0.0, rank.astype(jnp.int32), -1)


def hidden_kernel(
    place_ref, high_ref, low_ref, inner_ref, own_ref, other_ref, gate_ref,
    residual_ref, moe_gain_ref, router_ref, routes_ref, hidden_ref, stats_ref, *rest,
):
    packed_refs, rank_ref = rest[:-1], rest[-1]
    half = own_ref.shape[0]
    heads, length = 2 * half, inner_ref.shape[0]
    count, slots = len(packed_refs), packed_refs[0].shape[0]
    first_half = place_ref[0] % 2 == 0
    squares = jnp.zeros((length, LANES), F32)
    logits = jnp.zeros((count, length), F32)
    for h in range(heads):
        lanes = pl.ds(h * LANES, LANES)
        mine, other = own_ref[h % half], other_ref[pl.ds((h % half) * LANES, LANES), :]
        carry = jnp.where(first_half == (h < half), mine, other)
        attn = inner_ref[:, lanes] + (mm(high_ref[:, lanes], carry) + mm(low_ref[:, lanes], carry))
        mean_sq = jnp.mean(attn * attn, axis=1, keepdims=True)
        gated = attn * lax.rsqrt(mean_sq + 1e-06) * gate_ref[:, lanes]
        hidden = (residual_ref[:, lanes].astype(F32) + gated).astype(BF16)
        hidden_ref[:, lanes] = hidden
        wide = hidden.astype(F32)
        squares = squares + wide * wide
        scaled = (wide * moe_gain_ref[:, lanes].astype(F32)).astype(BF16)
        logits = logits + mm(router_ref[:, lanes], scaled, NT)
    stats_ref[0:count, :] = logits
    stats_ref[count:, :] = exact(jnp.ones((8, LANES), F32), squares, NT)
    _, _, rank = expert_table(routes_ref, count)
    rank_ref[...] = rank
    rows = hidden_ref[...]
    slot = lax.broadcasted_iota(jnp.int32, (slots, length), 0)
    for k, packed_ref in enumerate(packed_refs):
        pick = jnp.where(rank_ref[pl.ds(place_ref[0] ^ k, 1), :] == slot, 1.0, 0.0).astype(BF16)
        packed_ref[...] = mm(pick, rows).astype(BF16)


def rows_kernel(moe_gain_ref, *rest):
    arrived_refs, (rows_ref, squares_ref) = rest[:-2], rest[-2:]
    capacity, width = arrived_refs[0].shape
    total = len(arrived_refs) * capacity
    groups = pl.cdiv(total, LANES)
    sums = []
    for s, arrived_ref in enumerate(arrived_refs):
        wide = arrived_ref[...].astype(F32)
        rows_ref[pl.ds(s * capacity, capacity), :] = (wide * moe_gain_ref[...].astype(F32)).astype(BF16)
        square = wide * wide
        part = square[:, :LANES]
        for k in range(1, width // LANES):
            part = part + square[:, k * LANES : (k + 1) * LANES]
        sums.append(part)
    sums = jnp.concatenate(sums + [jnp.zeros((groups * LANES - total, LANES), F32)], axis=0)
    ones = jnp.ones((8, LANES), F32)
    lines = [exact(ones, sums[g * LANES : (g + 1) * LANES], NT)[0:1] for g in range(groups)]
    high, low = split2(jnp.concatenate(lines, axis=0))
    squares_ref[...] = jnp.concatenate(
        [high, low, jnp.zeros((PAD - 2 * groups, LANES), BF16)], axis=0
    )


def fetch_kernel(jobs, gate_ref, up_ref, down_ref, *rest):
    targets, sems = rest[:-1], rest[-1]
    copies = []
    for n, (which, start, size) in enumerate(jobs):
        if which == 2:
            source = down_ref.at[pl.ds(start, size), :]
        else:
            source = (gate_ref, up_ref)[which].at[:, pl.ds(start, size)]
        copies.append(pltpu.make_async_copy(source, targets[n], sems.at[n]))
    for copy in copies:
        copy.start()
    for copy in copies:
        copy.wait()


def chosen(place_ref, other_y, other_core):
    core, y = place_ref[0] % 2, place_ref[0] // 2
    return (1 - y if other_y else y) * 2 + (1 - core if other_core else core)


def up_part(home, extra, place_ref, rows_ref, squares_ref, *rest):
    if home:
        came_ref, gate_ref, up_ref, cross_ref, stay_ref, *more = rest
    else:
        gate_ref, up_ref, cross_ref = rest
    total = rows_ref.shape[0]
    piece = gate_ref.shape[1] // 4
    if extra:
        lines = squares_ref[...]
        if home:
            groups = pl.cdiv(total, LANES)
            seen = came_ref[pl.ds(total, PAD), pl.ds(0, LANES)].astype(F32) + lines.astype(F32)
            line_sum = seen[:groups] + seen[groups : 2 * groups]
            more[0][...] = jnp.concatenate([line_sum, jnp.zeros((PAD - groups, LANES), F32)], axis=0)
            high, low = split2(line_sum)
            lines = jnp.concatenate([high, low, jnp.zeros((PAD - 2 * groups, LANES), BF16)], axis=0)
        cross_ref[pl.ds(total, PAD), pl.ds(0, LANES)] = lines
        left = cross_ref.shape[1] - LANES
        cross_ref[pl.ds(total, PAD), pl.ds(LANES, left)] = jnp.zeros((PAD, left), BF16)
    for k in range(2):
        start = pl.multiple_of(chosen(place_ref, k == 0, not home) * piece, LANES)
        for i, weights in enumerate((gate_ref, up_ref)):
            lanes = pl.ds((2 * k + i) * piece, piece)
            sums = mm(rows_ref[...], weights[:, pl.ds(start, piece)])
            if home:
                sums = sums + came_ref[pl.ds(0, total), lanes].astype(F32)
            if home and k == 1:
                stay_ref[:, pl.ds(i * piece, piece)] = sums
            else:
                cross_ref[pl.ds(0, total), lanes] = sums.astype(BF16)


def up_kernel(jobs, place_ref, rows_ref, squares_ref, *refs):
    counts = [(3 if home else 2, 1 + home + (home and extra)) for home, extra in jobs]
    inputs, outputs = refs[: sum(n for n, _ in counts)], refs[sum(n for n, _ in counts) :]
    for (home, extra), (taken, made) in zip(jobs, counts):
        up_part(home, extra, place_ref, rows_ref, squares_ref, *inputs[:taken], *outputs[:made])
        inputs, outputs = inputs[taken:], outputs[made:]


def act_kernel(full_width, extra, stay_ref, seen_ref, scale_ref, act_ref, *more):
    total, piece = act_ref.shape
    if extra:
        groups = pl.cdiv(total, LANES)
        lines = seen_ref[pl.ds(total, PAD), pl.ds(0, LANES)].astype(F32)
        line_sum = scale_ref[0:groups, :] + lines[:groups] + lines[groups : 2 * groups]
        factor = lax.rsqrt(line_sum / full_width + 1e-06)
        columns = [jnp.transpose(jnp.broadcast_to(factor[g : g + 1], (8, LANES))) for g in range(groups)]
        scale = jnp.concatenate(columns, axis=0)[:total]
        more[0][...] = scale
        scale = scale[:, 0:1]
    else:
        scale = scale_ref[:, 0:1]
    joined = stay_ref[...] + seen_ref[pl.ds(0, total), :].astype(F32)
    act_ref[...] = (silu(scale * joined[:, :piece]) * (scale * joined[:, piece:])).astype(BF16)


def down_kernel(start, place_ref, *rest):
    acts, rest = rest[:4], rest[4:]
    total, (down_ref, *out_refs) = (None, rest) if start else (rest[0][...], rest[1:])
    piece = acts[0].shape[1]
    for n in range(4):
        row = pl.multiple_of(chosen(place_ref, n % 2 == 1, n >= 2) * piece, LANES)
        term = mm(acts[n][...], down_ref[pl.ds(row, piece), :])
        total = term if total is None else total + term
    if out_refs[0].dtype == F32:
        out_refs[0][...] = total
    else:
        for s, out_ref in enumerate(out_refs):
            capacity = out_ref.shape[0]
            out_ref[...] = total[s * capacity : (s + 1) * capacity].astype(BF16)


def combine_kernel(full_width, place_ref, hidden_ref, stats_ref, routes_ref, *rest):
    returned_refs, (out_ref, rank_ref, weight_ref) = rest[:-3], rest[-3:]
    count, slots = len(returned_refs), returned_refs[0].shape[0]
    length = hidden_ref.shape[0]
    first, second, rank_ref[...] = expert_table(routes_ref, count)
    scale = lax.rsqrt(stats_ref[count : count + 1, :] / full_width + 1e-06)
    logits = stats_ref[0:count, :] * scale
    gap = jnp.sum(jnp.where(first, logits, 0.0), axis=0, keepdims=True) - jnp.sum(
        jnp.where(second, logits, 0.0), axis=0, keepdims=True
    )
    weight_ref[...] = jnp.where(first, 1.0 / (1.0 + jnp.exp(-gap)), 1.0 / (1.0 + jnp.exp(gap)))
    slot = lax.broadcasted_iota(jnp.int32, (slots, length), 0)
    total = hidden_ref[...].astype(F32)
    for k, returned_ref in enumerate(returned_refs):
        line = pl.ds(place_ref[0] ^ k, 1)
        pick = jnp.where(rank_ref[line, :] == slot, weight_ref[line, :], 0.0)
        high, low = split2(pick)
        total = total + mm(high, returned_ref[...], TN) + mm(low, returned_ref[...], TN)
    out_ref[...] = total.astype(BF16)


LIGHT = 1
VMEM = pl.BlockSpec(memory_space=pltpu.VMEM)
SMEM = pl.BlockSpec(memory_space=pltpu.SMEM)
ANY = pl.BlockSpec(memory_space=pl.ANY)


def call(kernel, outs, specs, scratch=(), flops=0, moved=0, room=6):
    shapes = [jax.ShapeDtypeStruct(*out) for out in outs]
    single = len(shapes) == 1
    return pl.pallas_call(
        kernel,
        out_shape=shapes[0] if single else shapes,
        in_specs=specs,
        out_specs=VMEM if single else [VMEM] * len(shapes),
        scratch_shapes=list(scratch),
        cost_estimate=pl.CostEstimate(flops=flops // LIGHT, bytes_accessed=moved // LIGHT, transcendentals=0),
        compiler_params=pltpu.CompilerParams(vmem_limit_bytes=room << 20),
    )


def pinned(array):
    return pltpu.with_memory_space_constraint(array, pltpu.HBM)


def after_all(value, *others):
    return lax.optimization_barrier((value,) + others)[0]


def flip(count, bit):
    return [(i, i ^ bit) for i in range(count)]


def shift(count, step):
    return [(i, i + step) for i in range(count - step)]


def unpack(message, half):
    state = message[: half * LANES].astype(F32).reshape(half, LANES, LANES)
    lines = message[half * LANES :].astype(F32)
    return state, (lines[:half] + lines[half : 2 * half])[:, None, :]


def pack(state, decay):
    half = state.shape[0]
    return jnp.concatenate([state.astype(BF16).reshape(half * LANES, LANES), spread(decay[:, 0, :])])


UNITS = (3, 4, 2)
FETCH = tuple((name, c) for name in "gud" for c in range(len(UNITS)))
GROUPS = ((0, 1, 2, 3, 4, 5, 6, 7),)


def local_fast(
    queries, keys, values, log_decay, out_gate, attn_gain, residual, moe_gain, router, routes,
    w_gate, w_up, w_down,
):
    length, width = queries.shape
    heads = log_decay.shape[1]
    half = heads // 2
    spots, parts = lax.axis_size("seq"), lax.axis_size("head")
    place, part = lax.axis_index("seq"), lax.axis_index("head")
    count = router.shape[1]
    capacity = 2 * length // count + max(1, length // 32)
    hidden_units = w_gate.shape[1]
    decay_t, routes_t, router_t = log_decay.T, routes.T, router.T
    gain_row, moe_row = attn_gain.reshape(1, width), moe_gain.reshape(1, width)
    spot = place.astype(jnp.int32).reshape(1)

    head_flops = 2 * length * LANES * LANES * heads
    sent, kept, own_decay = call(
        state_kernel,
        [((half * LANES + PAD, LANES), BF16), ((half, LANES, LANES), F32), ((half, LANES), F32)],
        [SMEM, VMEM, VMEM, VMEM],
        [pltpu.VMEM((heads, LANES, LANES), F32), pltpu.VMEM((2, half, LANES), F32)],
        2 * head_flops,
        6 * length * width,
    )(spot, pinned(keys), pinned(values), decay_t)
    own_decay = own_decay[:, None, :]
    inner, query_high, query_low, gate = call(
        inner_kernel,
        [((length, width), F32), ((length, width), BF16), ((length, width), BF16), ((length, width), F32)],
        [VMEM] * 6,
        (),
        5 * head_flops,
        20 * length * width,
    )(pinned(queries), pinned(keys), pinned(values), decay_t, gain_row, pinned(out_gate))

    gates, ups, downs = {}, {}, {}

    def fetch(names, token):
        jobs, shapes = [], []
        for name, c in names:
            span = spans[c]
            size = span.stop - span.start
            jobs.append(("gud".index(name), span.start, size))
            shapes.append(pltpu.VMEM((size, width) if name == "d" else (width, size), BF16))
        moved = pl.pallas_call(
            functools.partial(fetch_kernel, jobs),
            out_shape=shapes,
            in_specs=[ANY] * 3,
            out_specs=[VMEM] * len(jobs),
            scratch_shapes=[pltpu.SemaphoreType.DMA((len(jobs),))],
            cost_estimate=pl.CostEstimate(flops=0, bytes_accessed=1 << 20, transcendentals=0),
            compiler_params=pltpu.CompilerParams(vmem_limit_bytes=2 << 20),
        )(*[pinned(after_all(w, token)) for w in (w_gate, w_up, w_down)])
        for (name, c), array in zip(names, moved):
            {"g": gates, "u": ups, "d": downs}[name][c] = array
        return moved[0]

    even = place % 2 == 0
    part = part.astype(jnp.int32).reshape(1)
    chunks = range(len(UNITS))
    ends = [sum(UNITS[: c + 1]) * parts * LANES for c in chunks]
    spans = [slice(ends[c - 1] if c else 0, ends[c]) for c in chunks]

    theirs, their_decay = unpack(lax.ppermute(sent, "seq", flip(spots, 1)), half)
    kept = after_all(kept, inner)
    block = jnp.where(even, their_decay, 1.0) * kept + jnp.where(even, 1.0, own_decay) * theirs
    block_decay = own_decay * their_decay
    carry, between = jnp.zeros_like(block), jnp.ones_like(block_decay)
    step = 1
    while 2 * step < spots:
        window = pack(block + block_decay * carry, block_decay * between)
        if step == 1:
            window = after_all(window, moe_row)
        got, got_decay = unpack(lax.ppermute(window, "seq", shift(spots, 2 * step)), half)
        carry, between = carry + between * got, between * got_decay
        step *= 2
    after = jnp.where(even, own_decay, their_decay) * carry + jnp.where(even, kept, theirs)
    mine = jnp.where(even, carry, after).astype(BF16)
    other = jnp.where(even, after, carry).astype(BF16).reshape(half * LANES, LANES)
    other = lax.ppermute(other, "seq", flip(spots, 1))

    hidden, stats, *packed = call(
        hidden_kernel,
        [((length, width), BF16), ((count + 8, length), F32)] + [((capacity, width), BF16)] * spots,
        [SMEM] + [VMEM] * 10,
        [pltpu.VMEM((count, length), jnp.int32)],
        3 * head_flops,
        16 * length * width,
    )(
        spot, query_high, query_low, inner, mine, other, gate, pinned(residual),
        moe_row, pinned(router_t), pinned(routes_t),
    )
    def exchange(block, k):
        return lax.ppermute(block, "seq", flip(spots, k)) if k else block

    arrived = [exchange(block, k) for k, block in enumerate(packed)]
    sizes = [capacity * len(group) for group in GROUPS]
    pieces = [size * LANES for size in UNITS]
    state = {}
    turn = [hidden]

    def next_turn(value):
        return after_all(value, turn[-1])

    def gather(g):
        rows, squares = call(
            rows_kernel,
            [((sizes[g], width), BF16), ((PAD, LANES), BF16)],
            [VMEM] * (1 + len(GROUPS[g])),
            (),
            0,
            4 * sizes[g] * width,
        )(next_turn(moe_row), *[arrived[k] for k in GROUPS[g]])
        state["rows", g], state["squares", g] = rows, squares
        turn.append(rows)

    def up(g, *parts_of):
        size = sizes[g]
        outs, inputs, jobs = [], [], []
        for c, home in parts_of:
            extra, piece = c == 0, pieces[c]
            outs.append(((size + PAD * extra, (2 if home else 4) * piece), BF16))
            if home:
                outs.append(((size, 2 * piece), F32))
                inputs.append(state["came", g, c])
                if extra:
                    outs.append(((PAD, LANES), F32))
            inputs += [gates[c], ups[c]]
            jobs.append((home, extra))
        made = call(
            functools.partial(up_kernel, jobs),
            outs,
            [SMEM] + [VMEM] * (2 + len(inputs)),
            (),
            8 * size * width * sum(pieces[c] for c, _ in parts_of),
            8 * size * width,
        )(part, next_turn(state["rows", g]), state["squares", g], *inputs)
        made = [made] if len(outs) == 1 else list(made)
        turn.append(made[0])
        for (c, home), (_, extra) in zip(parts_of, jobs):
            cross = made.pop(0)
            if home:
                state["stay", g, c] = made.pop(0)
                if extra:
                    state["lines", g] = made.pop(0)
                state["seen", g, c] = lax.ppermute(cross, "head", flip(parts, 2))
            else:
                state["came", g, c] = lax.ppermute(cross, "head", flip(parts, 1))

    def act(g, c):
        size, piece, extra = sizes[g], pieces[c], c == 0
        made = call(
            functools.partial(act_kernel, float(width * parts), extra),
            [((size, piece), BF16)] + [((size, 8), F32)] * extra,
            [VMEM] * 3,
            (),
            0,
            10 * size * piece,
        )(
            next_turn(state["stay", g, c]),
            state["seen", g, c],
            state["lines" if extra else "scale", g],
        )
        if extra:
            made, state["scale", g] = made
        across = lax.ppermute(made, "head", flip(parts, 2))
        beside = lax.ppermute(made, "head", flip(parts, 1))
        state["acts", g, c] = [made, across, beside]
        turn.append(made)

    def down(g, c):
        size, piece, last = sizes[g], pieces[c], c == chunks[-1]
        made, across, beside = state["acts", g, c]
        diagonal = lax.ppermute(across, "head", flip(parts, 1))
        acc = state.get(("acc", g))
        out = call(
            functools.partial(down_kernel, c == 0),
            [((capacity, width), BF16)] * len(GROUPS[g]) if last else [((size, width), F32)],
            [SMEM] + [VMEM] * (5 + (c > 0)),
            (),
            8 * size * width * piece,
            8 * size * width,
        )(part, next_turn(made), across, beside, diagonal, *([acc] if c else []), downs[c])
        state["acc", g] = out
        turn.append(out[0] if last else out)
        if last:
            for k, block in zip(GROUPS[g], out):
                returned[k] = exchange(block, k)

    def late_fetch():
        turn.append(fetch(FETCH, turn[-1]))

    returned = {}
    for job, *where in PLAN:
        {"gather": gather, "up": up, "act": act, "down": down, "fetch": late_fetch}[job](*where)
    stats = lax.psum(next_turn(stats), "head")
    return call(
        functools.partial(combine_kernel, float(width * parts)),
        [((length, width), BF16)],
        [SMEM] + [VMEM] * (3 + spots),
        [pltpu.VMEM((count, length), jnp.int32), pltpu.VMEM((count, length), F32)],
        4 * length * count * capacity * width,
        8 * length * width,
    )(spot, hidden, stats, pinned(routes_t), *[returned[k] for k in range(spots)])


PLAN = (
    ("fetch",),
    ("gather", 0),
    ("up", 0, (0, False)),
    ("up", 0, (0, True), (1, False)),
    ("up", 0, (1, True), (2, False)),
    ("up", 0, (2, True)),
    ("act", 0, 0),
    ("act", 0, 1),
    ("act", 0, 2),
    ("down", 0, 0),
    ("down", 0, 1),
    ("down", 0, 2),
)


def local(*args):
    queries, log_decay, router, w_gate = args[0], args[3], args[8], args[10]
    spots, parts = lax.axis_size("seq"), lax.axis_size("head")
    heads = log_decay.shape[1]
    fits = (
        router.shape[1] == spots == sum(map(len, GROUPS))
        and parts == 4
        and heads % 2 == 0
        and queries.shape == (LANES, heads * LANES)
        and w_gate.shape[1] == sum(UNITS) * parts * LANES
    )
    return local_fast(*args) if fits else local_general(*args)


def solution(mesh):
    return jax.shard_map(
        local,
        mesh=mesh,
        in_specs=(
            P("seq", "head"),
            P("seq", "head"),
            P("seq", "head"),
            P("seq", "head"),
            P("seq", "head"),
            P("head"),
            P("seq", "head"),
            P("head"),
            P("head", None),
            P("seq", None),
            P("head", "seq"),
            P("head", "seq"),
            P("seq", "head"),
        ),
        out_specs=P("seq", "head"),
        check_vma=False,
    )
```

```python
import functools

import jax
import jax.numpy as jnp
from jax import lax
from jax.experimental import pallas as pl
from jax.experimental.pallas import tpu as pltpu
from jax.sharding import PartitionSpec as P


def prefix_2(value, axis, join, neutral):
    count, mine = (lax.axis_size(axis), lax.axis_index(axis))
    pieces = jax.tree.map(lambda part: lax.all_gather(part, axis), value)
    subtotal = jax.tree.map(
        lambda part, zero: jnp.full_like(part, 0) + jnp.asarray(zero, part.dtype), value, neutral
    )

    def lap(position, subtotal):
        longer = join(subtotal, jax.tree.map(lambda part: part[position], pieces))
        return jax.tree.map(lambda new, old: jnp.where(position < mine, new, old), longer, subtotal)

    return lax.fori_loop(0, count - 1, lap, subtotal)


def block_terms(query_act, key_act, value_all, decay_log):
    length = query_act.shape[0]
    cumulative = jnp.cumsum(decay_log, axis=0)
    row_index = lax.broadcasted_iota(jnp.int32, (length, length), 0)
    col_index = lax.broadcasted_iota(jnp.int32, (length, length), 1)
    causal = (row_index >= col_index)[None, :, :]
    by_head = jnp.transpose(cumulative)
    spread = by_head[:, :, None] - by_head[:, None, :]
    weight = jnp.where(causal, jnp.exp(jnp.where(causal, spread, 0.0)), 0.0)
    scores = (
        jnp.einsum("ihe,jhe->hij", query_act, key_act, precision=lax.Precision.HIGHEST) * weight
    )
    inner_part = jnp.einsum("hij,jhe->ihe", scores, value_all, precision=lax.Precision.HIGHEST)
    tail_decay = jnp.exp(cumulative[-1][None, :] - cumulative)
    local_state = jnp.einsum(
        "jhe,jhf->hef", key_act * tail_decay[:, :, None], value_all, precision=lax.Precision.HIGHEST
    )
    return (cumulative, inner_part, local_state, jnp.exp(cumulative[-1]))


def attention_out(inner_part, cumulative, carry_state, query_act):
    earlier = jnp.einsum("ihe,hef->ihf", query_act, carry_state, precision=lax.Precision.HIGHEST)
    return inner_part + jnp.exp(cumulative)[:, :, None] * earlier


def finish(attn, attn_gain, out_gate, residual):
    mean_sq = jnp.mean(attn * attn, axis=-1, keepdims=True)
    normed_heads = attn * lax.rsqrt(mean_sq + 1e-06)
    flat = normed_heads.reshape(attn.shape[0], attn.shape[1] * attn.shape[2])
    gated = flat * attn_gain.astype(jnp.float32) * jax.nn.sigmoid(out_gate.astype(jnp.float32))
    return (residual.astype(jnp.float32) + gated).astype(jnp.bfloat16)


def gate_weights(logits, routes):
    expert_ids = lax.broadcasted_iota(jnp.int32, (1, 1, logits.shape[1]), 2)
    onehot = routes[:, :, None] == expert_ids
    picked = jnp.sum(jnp.where(onehot, logits[:, None, :], 0.0), axis=-1)
    return jax.nn.sigmoid(picked - picked[:, ::-1])


def slot_table(routes, expert_count, capacity):
    flat_ids = routes.reshape(-1)
    expert_ids = lax.broadcasted_iota(jnp.int32, (1, expert_count), 1)
    onehot = (flat_ids[:, None] == expert_ids).astype(jnp.int32)
    ranking = jnp.cumsum(onehot, axis=0) - onehot
    own_rank = jnp.sum(ranking * onehot, axis=1)
    slot_ids = flat_ids * capacity + own_rank
    slot_range = lax.broadcasted_iota(jnp.int32, (1, expert_count * capacity), 1)
    return (slot_ids[:, None] == slot_range).astype(jnp.float32)


def build_sends(tok_rows, slot_bf16, expert_count, capacity, owner_count):
    doubled = jnp.repeat(tok_rows, 2, axis=0)
    packed = jnp.einsum("as,ad->sd", slot_bf16, doubled, preferred_element_type=jnp.float32).astype(
        jnp.bfloat16
    )
    width = tok_rows.shape[1]
    fanned = jnp.broadcast_to(
        packed.reshape(expert_count, 1, capacity, width),
        (expert_count, owner_count, capacity, width),
    )
    return fanned.reshape(expert_count * owner_count, capacity, width)


def local_general(
    queries,
    keys,
    values,
    log_decay,
    out_gate,
    attn_gain,
    residual,
    moe_gain,
    router,
    routes,
    w_gate,
    w_up,
    w_down,
):
    tok_count = queries.shape[0]
    heads_here = log_decay.shape[1]
    head_size = queries.shape[1] // heads_here
    query_act = jax.nn.silu(queries.astype(jnp.float32)).reshape(tok_count, heads_here, head_size)
    key_act = jax.nn.silu(keys.astype(jnp.float32)).reshape(tok_count, heads_here, head_size)
    value_all = values.astype(jnp.float32).reshape(tok_count, heads_here, head_size)
    cumulative, inner_part, local_state, block_decay = block_terms(
        query_act, key_act, value_all, log_decay
    )

    def combine(earlier, later):
        return (earlier[0] * later[0], later[0][:, None, None] * earlier[1] + later[1])

    identity = (jnp.ones_like(block_decay), jnp.zeros_like(local_state))
    prefix = prefix_2((block_decay, local_state), "seq", combine, identity)
    attn = attention_out(inner_part, cumulative, prefix[1], query_act)
    hidden = finish(attn, attn_gain, out_gate, residual)
    part_width = hidden.shape[1]
    full_width = part_width * lax.axis_size("head")
    wide = hidden.astype(jnp.float32)
    squares = lax.psum(jnp.sum(wide * wide, axis=1), "head")
    scale = lax.rsqrt(squares / full_width + 1e-06)
    normed = (wide * scale[:, None] * moe_gain.astype(jnp.float32)).astype(jnp.bfloat16)
    logits = lax.psum(jnp.dot(normed, router, preferred_element_type=jnp.float32), "head")
    weights = gate_weights(logits, routes)
    expert_count = router.shape[1]
    owner_count = lax.axis_size("seq") // expert_count
    capacity = 2 * tok_count // expert_count + max(1, tok_count // 32)
    table = slot_table(routes, expert_count, capacity)
    outgoing = build_sends(normed, table.astype(jnp.bfloat16), expert_count, capacity, owner_count)
    arrived = lax.all_to_all(outgoing, "seq", split_axis=0, concat_axis=0, tiled=True)
    sources, items, width = arrived.shape
    flat_rows = arrived.reshape(sources * items, width)
    gate_part = jnp.dot(flat_rows, w_gate, preferred_element_type=jnp.float32)
    up_part = jnp.dot(flat_rows, w_up, preferred_element_type=jnp.float32)
    gate = lax.psum_scatter(gate_part, "head", scatter_dimension=1, tiled=True)
    upward = lax.psum_scatter(up_part, "head", scatter_dimension=1, tiled=True)
    act = (jax.nn.silu(gate) * upward).astype(jnp.bfloat16)
    act = lax.all_gather(act, "head", axis=1, tiled=True)
    result = jnp.dot(act, w_down, preferred_element_type=jnp.float32).astype(jnp.bfloat16)
    shares = result.reshape(sources, items, width)
    returned = lax.all_to_all(shares, "seq", split_axis=0, concat_axis=0, tiled=True)
    summed = (
        returned.astype(jnp.float32)
        .reshape(expert_count, owner_count, capacity, part_width)
        .sum(axis=1)
    )
    summed = summed.reshape(expert_count * capacity, part_width)
    per_token = (
        (table * weights.reshape(-1)[:, None])
        .reshape(tok_count, 2, expert_count * capacity)
        .sum(axis=1)
    )
    moe = jnp.dot(per_token, summed, precision=lax.Precision.HIGHEST)
    return (hidden.astype(jnp.float32) + moe).astype(jnp.bfloat16)


F32, BF16 = jnp.float32, jnp.bfloat16
LANES = 128
PAD = 16
NT = (((1,), (1,)), ((), ()))
TN = (((0,), (0,)), ((), ()))


def mm(a, b, dims=(((1,), (0,)), ((), ()))):
    return lax.dot_general(a, b, dims, preferred_element_type=F32)


def exact(a, b, dims=(((1,), (0,)), ((), ()))):
    return lax.dot_general(
        a, b, dims, preferred_element_type=F32, precision=lax.Precision.HIGHEST
    )


def split2(a):
    high = a.astype(BF16)
    return high, (a - high.astype(F32)).astype(BF16)


def silu(a):
    return a / (1.0 + jnp.exp(-a))


def decay_rows(decay_ref):
    heads, length = decay_ref.shape
    row = lax.broadcasted_iota(jnp.int32, (length, length), 0)
    col = lax.broadcasted_iota(jnp.int32, (length, length), 1)
    return exact(decay_ref[...], (row <= col).astype(F32)), row, col


def spread(values):
    high, low = split2(jnp.broadcast_to(values, (values.shape[0], LANES)))
    rest = PAD - 2 * values.shape[0]
    return jnp.concatenate([high, low, jnp.zeros((rest, LANES), BF16)], axis=0)


def state_kernel(place_ref, keys_ref, values_ref, decay_ref, sent_ref, kept_ref, own_ref, all_ref, dec_ref):
    heads, length = decay_ref.shape
    half = heads // 2
    cum, _, _ = decay_rows(decay_ref)
    total = cum[:, length - 1 :]
    tail = jnp.transpose(jnp.exp(total - cum))
    whole = jnp.exp(total)
    for h in range(heads):
        lanes = pl.ds(h * LANES, LANES)
        act = silu(keys_ref[:, lanes].astype(F32)) * tail[:, h : h + 1]
        high, low = split2(act)
        value = values_ref[:, lanes]
        all_ref[h] = mm(high, value, TN) + mm(low, value, TN)
    dec_ref[0] = jnp.broadcast_to(whole[:half], (half, LANES))
    dec_ref[1] = jnp.broadcast_to(whole[half:], (half, LANES))
    mine = place_ref[0] % 2
    for i in range(half):
        sent_ref[pl.ds(i * LANES, LANES), :] = all_ref[(1 - mine) * half + i].astype(BF16)
        kept_ref[i] = all_ref[mine * half + i]
    sent_ref[pl.ds(half * LANES, PAD), :] = spread(dec_ref[1 - mine])
    own_ref[...] = dec_ref[mine]


def inner_kernel(
    queries_ref, keys_ref, values_ref, decay_ref, inner_ref, high_ref, low_ref
):
    heads, length = decay_ref.shape
    cum, row, col = decay_rows(decay_ref)
    columns = jnp.transpose(cum)
    grown = jnp.exp(columns)
    causal = row >= col
    for h in range(heads):
        lanes = pl.ds(h * LANES, LANES)
        query = silu(queries_ref[:, lanes].astype(F32))
        high_ref[:, lanes], low_ref[:, lanes] = split2(query * grown[:, h : h + 1])
        q_high, q_low = split2(query)
        k_high, k_low = split2(silu(keys_ref[:, lanes].astype(F32)))
        gap = jnp.where(causal, columns[:, h : h + 1] - cum[h : h + 1, :], 0.0)
        weight = jnp.where(causal, jnp.exp(gap), 0.0)
        scores = (mm(q_high, k_high, NT) + (mm(q_high, k_low, NT) + mm(q_low, k_high, NT))) * weight
        high, low = split2(scores)
        value = values_ref[:, lanes]
        inner_ref[:, lanes] = mm(high, value) + mm(low, value)


def gate_kernel(gain_ref, gate_ref, out_ref):
    gate = 1.0 / (1.0 + jnp.exp(-gate_ref[...].astype(F32)))
    out_ref[...] = gate * gain_ref[...].astype(F32)


def expert_table(routes_ref, count):
    length = routes_ref.shape[1]
    ids = lax.broadcasted_iota(jnp.int32, (count, length), 0)
    first = routes_ref[0:1, :] == ids
    second = routes_ref[1:2, :] == ids
    named = jnp.where(first | second, 1.0, 0.0)
    row = lax.broadcasted_iota(jnp.int32, (length, length), 0)
    col = lax.broadcasted_iota(jnp.int32, (length, length), 1)
    rank = mm(named.astype(BF16), jnp.where(row < col, 1.0, 0.0).astype(BF16))
    return first, second, jnp.where(named > 0.0, rank.astype(jnp.int32), -1)


def hidden_kernel(
    place_ref, high_ref, low_ref, inner_ref, own_ref, other_ref, gate_ref,
    residual_ref, moe_gain_ref, router_ref, routes_ref, hidden_ref, stats_ref, *rest,
):
    packed_refs, rank_ref = rest[:-1], rest[-1]
    half = own_ref.shape[0]
    heads, length = 2 * half, inner_ref.shape[0]
    count, slots = len(packed_refs), packed_refs[0].shape[0]
    first_half = place_ref[0] % 2 == 0
    squares = jnp.zeros((length, LANES), F32)
    logits = jnp.zeros((count, length), F32)
    for h in range(heads):
        lanes = pl.ds(h * LANES, LANES)
        mine, other = own_ref[h % half], other_ref[pl.ds((h % half) * LANES, LANES), :]
        carry = jnp.where(first_half == (h < half), mine, other)
        attn = inner_ref[:, lanes] + (mm(high_ref[:, lanes], carry) + mm(low_ref[:, lanes], carry))
        mean_sq = jnp.mean(attn * attn, axis=1, keepdims=True)
        gated = attn * lax.rsqrt(mean_sq + 1e-06) * gate_ref[:, lanes]
        hidden = (residual_ref[:, lanes].astype(F32) + gated).astype(BF16)
        hidden_ref[:, lanes] = hidden
        wide = hidden.astype(F32)
        squares = squares + wide * wide
        scaled = (wide * moe_gain_ref[:, lanes].astype(F32)).astype(BF16)
        logits = logits + mm(router_ref[:, lanes], scaled, NT)
    stats_ref[0:count, :] = logits
    stats_ref[count:, :] = exact(jnp.ones((8, LANES), F32), squares, NT)
    _, _, rank = expert_table(routes_ref, count)
    rank_ref[...] = rank
    rows = hidden_ref[...]
    slot = lax.broadcasted_iota(jnp.int32, (slots, length), 0)
    for k, packed_ref in enumerate(packed_refs):
        pick = jnp.where(rank_ref[pl.ds(place_ref[0] ^ k, 1), :] == slot, 1.0, 0.0).astype(BF16)
        packed_ref[...] = mm(pick, rows).astype(BF16)


def rows_kernel(moe_gain_ref, *rest):
    arrived_refs, (rows_ref, squares_ref) = rest[:-2], rest[-2:]
    capacity, width = arrived_refs[0].shape
    total = len(arrived_refs) * capacity
    groups = pl.cdiv(total, LANES)
    sums = []
    for s, arrived_ref in enumerate(arrived_refs):
        wide = arrived_ref[...].astype(F32)
        rows_ref[pl.ds(s * capacity, capacity), :] = (wide * moe_gain_ref[...].astype(F32)).astype(BF16)
        square = wide * wide
        part = square[:, :LANES]
        for k in range(1, width // LANES):
            part = part + square[:, k * LANES : (k + 1) * LANES]
        sums.append(part)
    sums = jnp.concatenate(sums + [jnp.zeros((groups * LANES - total, LANES), F32)], axis=0)
    ones = jnp.ones((8, LANES), F32)
    lines = [exact(ones, sums[g * LANES : (g + 1) * LANES], NT)[0:1] for g in range(groups)]
    high, low = split2(jnp.concatenate(lines, axis=0))
    squares_ref[...] = jnp.concatenate(
        [high, low, jnp.zeros((PAD - 2 * groups, LANES), BF16)], axis=0
    )


def fetch_kernel(jobs, gate_ref, up_ref, down_ref, *rest):
    targets, sems = rest[:-1], rest[-1]
    copies = []
    for n, (which, start, size) in enumerate(jobs):
        if which == 2:
            source = down_ref.at[pl.ds(start, size), :]
        else:
            source = (gate_ref, up_ref)[which].at[:, pl.ds(start, size)]
        copies.append(pltpu.make_async_copy(source, targets[n], sems.at[n]))
    for copy in copies:
        copy.start()
    for copy in copies:
        copy.wait()


def chosen(place_ref, other_y, other_core):
    core, y = place_ref[0] % 2, place_ref[0] // 2
    return (1 - y if other_y else y) * 2 + (1 - core if other_core else core)


def up_part(home, place_ref, rows_ref, gate_ref, up_ref, out_ref):
    piece = gate_ref.shape[1] // 4
    for k in range(2):
        start = pl.multiple_of(chosen(place_ref, k == 0, not home) * piece, LANES)
        for i, weights in enumerate((gate_ref, up_ref)):
            lanes = pl.ds((2 * k + i) * piece, piece)
            sums = mm(rows_ref[...], weights[:, pl.ds(start, piece)])
            out_ref[pl.ds(0, rows_ref.shape[0]), lanes] = sums.astype(out_ref.dtype)


def up_kernel(jobs, place_ref, rows_ref, squares_ref, *refs):
    total = rows_ref.shape[0]
    for n, (home, extra) in enumerate(jobs):
        out_ref = refs[2 * len(jobs) + n]
        if extra:
            left = out_ref.shape[1] - LANES
            out_ref[pl.ds(total, PAD), pl.ds(0, LANES)] = squares_ref[...]
            out_ref[pl.ds(total, PAD), pl.ds(LANES, left)] = jnp.zeros((PAD, left), BF16)
        up_part(home, place_ref, rows_ref, refs[2 * n], refs[2 * n + 1], out_ref)


def add_kernel(extra, home_ref, came_ref, squares_ref, cross_ref, stay_ref, *more):
    total, width = stay_ref.shape
    for k in range(2):
        lanes = pl.ds(k * width, width)
        sums = home_ref[:, lanes] + came_ref[pl.ds(0, total), lanes].astype(F32)
        if k:
            stay_ref[...] = sums
        else:
            cross_ref[pl.ds(0, total), :] = sums.astype(BF16)
    if extra:
        groups = pl.cdiv(total, LANES)
        seen = came_ref[pl.ds(total, PAD), pl.ds(0, LANES)].astype(F32) + squares_ref[...].astype(F32)
        line_sum = seen[:groups] + seen[groups : 2 * groups]
        more[0][...] = jnp.concatenate([line_sum, jnp.zeros((PAD - groups, LANES), F32)], axis=0)
        high, low = split2(line_sum)
        lines = jnp.concatenate([high, low, jnp.zeros((PAD - 2 * groups, LANES), BF16)], axis=0)
        cross_ref[pl.ds(total, PAD), pl.ds(0, LANES)] = lines
        cross_ref[pl.ds(total, PAD), pl.ds(LANES, width - LANES)] = jnp.zeros((PAD, width - LANES), BF16)


def act_kernel(full_width, extra, stay_ref, seen_ref, scale_ref, act_ref, *more):
    total, piece = act_ref.shape
    if extra:
        groups = pl.cdiv(total, LANES)
        lines = seen_ref[pl.ds(total, PAD), pl.ds(0, LANES)].astype(F32)
        line_sum = scale_ref[0:groups, :] + lines[:groups] + lines[groups : 2 * groups]
        factor = lax.rsqrt(line_sum / full_width + 1e-06)
        columns = [jnp.transpose(jnp.broadcast_to(factor[g : g + 1], (8, LANES))) for g in range(groups)]
        scale = jnp.concatenate(columns, axis=0)[:total]
        more[0][...] = scale
        scale = scale[:, 0:1]
    else:
        scale = scale_ref[:, 0:1]
    joined = stay_ref[...] + seen_ref[pl.ds(0, total), :].astype(F32)
    act_ref[...] = (silu(scale * joined[:, :piece]) * (scale * joined[:, piece:])).astype(BF16)


def down_kernel(start, place_ref, *rest):
    acts, rest = rest[:4], rest[4:]
    total, (down_ref, *out_refs) = (None, rest) if start else (rest[0][...], rest[1:])
    piece = acts[0].shape[1]
    for n in range(4):
        row = pl.multiple_of(chosen(place_ref, n % 2 == 1, n >= 2) * piece, LANES)
        term = mm(acts[n][...], down_ref[pl.ds(row, piece), :])
        total = term if total is None else total + term
    if out_refs[0].dtype == F32:
        out_refs[0][...] = total
    else:
        for s, out_ref in enumerate(out_refs):
            capacity = out_ref.shape[0]
            out_ref[...] = total[s * capacity : (s + 1) * capacity].astype(BF16)


def combine_kernel(full_width, place_ref, hidden_ref, stats_ref, routes_ref, *rest):
    returned_refs, (out_ref, rank_ref, weight_ref) = rest[:-3], rest[-3:]
    count, slots = len(returned_refs), returned_refs[0].shape[0]
    length = hidden_ref.shape[0]
    first, second, rank_ref[...] = expert_table(routes_ref, count)
    scale = lax.rsqrt(stats_ref[count : count + 1, :] / full_width + 1e-06)
    logits = stats_ref[0:count, :] * scale
    gap = jnp.sum(jnp.where(first, logits, 0.0), axis=0, keepdims=True) - jnp.sum(
        jnp.where(second, logits, 0.0), axis=0, keepdims=True
    )
    weight_ref[...] = jnp.where(first, 1.0 / (1.0 + jnp.exp(-gap)), 1.0 / (1.0 + jnp.exp(gap)))
    slot = lax.broadcasted_iota(jnp.int32, (slots, length), 0)
    total = hidden_ref[...].astype(F32)
    for k, returned_ref in enumerate(returned_refs):
        line = pl.ds(place_ref[0] ^ k, 1)
        pick = jnp.where(rank_ref[line, :] == slot, weight_ref[line, :], 0.0)
        high, low = split2(pick)
        total = total + mm(high, returned_ref[...], TN) + mm(low, returned_ref[...], TN)
    out_ref[...] = total.astype(BF16)


LIGHT = 1
VMEM = pl.BlockSpec(memory_space=pltpu.VMEM)
SMEM = pl.BlockSpec(memory_space=pltpu.SMEM)
ANY = pl.BlockSpec(memory_space=pl.ANY)


def call(kernel, outs, specs, scratch=(), flops=0, moved=0, room=6):
    shapes = [jax.ShapeDtypeStruct(*out) for out in outs]
    single = len(shapes) == 1
    return pl.pallas_call(
        kernel,
        out_shape=shapes[0] if single else shapes,
        in_specs=specs,
        out_specs=VMEM if single else [VMEM] * len(shapes),
        scratch_shapes=list(scratch),
        cost_estimate=pl.CostEstimate(flops=flops // LIGHT, bytes_accessed=moved // LIGHT, transcendentals=0),
        compiler_params=pltpu.CompilerParams(vmem_limit_bytes=room << 20),
    )


def pinned(array):
    return pltpu.with_memory_space_constraint(array, pltpu.HBM)


def after_all(value, *others):
    return lax.optimization_barrier((value,) + others)[0]


def flip(count, bit):
    return [(i, i ^ bit) for i in range(count)]


def shift(count, step):
    return [(i, i + step) for i in range(count - step)]


def unpack(message, half):
    state = message[: half * LANES].astype(F32).reshape(half, LANES, LANES)
    lines = message[half * LANES :].astype(F32)
    return state, (lines[:half] + lines[half : 2 * half])[:, None, :]


def pack(state, decay):
    half = state.shape[0]
    return jnp.concatenate([state.astype(BF16).reshape(half * LANES, LANES), spread(decay[:, 0, :])])


UNITS = (2, 4, 3)
FETCHES = tuple(tuple((name, c) for name in names for c in range(len(UNITS))) for names in ("gu", "d"))
GROUPS = ((0, 1, 2, 3, 4, 5, 6, 7),)


def local_fast(
    queries, keys, values, log_decay, out_gate, attn_gain, residual, moe_gain, router, routes,
    w_gate, w_up, w_down,
):
    length, width = queries.shape
    heads = log_decay.shape[1]
    half = heads // 2
    spots, parts = lax.axis_size("seq"), lax.axis_size("head")
    place, part = lax.axis_index("seq"), lax.axis_index("head")
    count = router.shape[1]
    capacity = 2 * length // count + max(1, length // 32)
    hidden_units = w_gate.shape[1]
    decay_t, routes_t, router_t = log_decay.T, routes.T, router.T
    spot = place.astype(jnp.int32).reshape(1)

    head_flops = 2 * length * LANES * LANES * heads
    sent, kept, own_decay = call(
        state_kernel,
        [((half * LANES + PAD, LANES), BF16), ((half, LANES, LANES), F32), ((half, LANES), F32)],
        [SMEM, VMEM, VMEM, VMEM],
        [pltpu.VMEM((heads, LANES, LANES), F32), pltpu.VMEM((2, half, LANES), F32)],
        2 * head_flops,
        6 * length * width,
    )(spot, pinned(keys), pinned(values), decay_t)
    own_decay = own_decay[:, None, :]
    inner, query_high, query_low = call(
        inner_kernel,
        [((length, width), F32), ((length, width), BF16), ((length, width), BF16)],
        [VMEM] * 4,
        (),
        5 * head_flops,
        16 * length * width,
    )(pinned(queries), pinned(keys), pinned(values), decay_t)

    gates, ups, downs = {}, {}, {}

    def fetch(names, token):
        jobs, shapes = [], []
        for name, c in names:
            span = spans[c]
            size = span.stop - span.start
            jobs.append(("gud".index(name), span.start, size))
            shapes.append(pltpu.VMEM((size, width) if name == "d" else (width, size), BF16))
        moved = pl.pallas_call(
            functools.partial(fetch_kernel, jobs),
            out_shape=shapes,
            in_specs=[ANY] * 3,
            out_specs=[VMEM] * len(jobs),
            scratch_shapes=[pltpu.SemaphoreType.DMA((len(jobs),))],
            cost_estimate=pl.CostEstimate(flops=0, bytes_accessed=1 << 20, transcendentals=0),
            compiler_params=pltpu.CompilerParams(vmem_limit_bytes=2 << 20),
        )(*[pinned(after_all(w, token)) for w in (w_gate, w_up, w_down)])
        for (name, c), array in zip(names, moved):
            {"g": gates, "u": ups, "d": downs}[name][c] = array
        return moved[0]

    even = place % 2 == 0
    part = part.astype(jnp.int32).reshape(1)
    chunks = range(len(UNITS))
    ends = [sum(UNITS[: c + 1]) * parts * LANES for c in chunks]
    spans = [slice(ends[c - 1] if c else 0, ends[c]) for c in chunks]

    theirs, their_decay = unpack(lax.ppermute(sent, "seq", flip(spots, 1)), half)
    kept = after_all(kept, inner)
    block = jnp.where(even, their_decay, 1.0) * kept + jnp.where(even, 1.0, own_decay) * theirs
    block_decay = own_decay * their_decay
    carry, between = jnp.zeros_like(block), jnp.ones_like(block_decay)
    step = 1
    while 2 * step < spots:
        window = pack(block + block_decay * carry, block_decay * between)
        if step == 1:
            gain_row = after_all(attn_gain, window).reshape(1, width)
            moe_row = after_all(moe_gain, window).reshape(1, width)
            gate = call(gate_kernel, [((length, width), F32)], [VMEM] * 2, (), 0, 6 * length * width)(
                gain_row, pinned(out_gate)
            )
        if step == 2:
            window = after_all(window, gate, moe_row)
        got, got_decay = unpack(lax.ppermute(window, "seq", shift(spots, 2 * step)), half)
        carry, between = carry + between * got, between * got_decay
        step *= 2
    after = jnp.where(even, own_decay, their_decay) * carry + jnp.where(even, kept, theirs)
    mine = jnp.where(even, carry, after).astype(BF16)
    other = jnp.where(even, after, carry).astype(BF16).reshape(half * LANES, LANES)
    other = lax.ppermute(other, "seq", flip(spots, 1))

    hidden, stats, *packed = call(
        hidden_kernel,
        [((length, width), BF16), ((count + 8, length), F32)] + [((capacity, width), BF16)] * spots,
        [SMEM] + [VMEM] * 10,
        [pltpu.VMEM((count, length), jnp.int32)],
        3 * head_flops,
        16 * length * width,
    )(
        spot, query_high, query_low, inner, mine, other, gate, pinned(residual),
        moe_row, pinned(router_t), pinned(routes_t),
    )
    def exchange(block, k):
        return lax.ppermute(block, "seq", flip(spots, k)) if k else block

    arrived = [exchange(block, k) for k, block in enumerate(packed)]
    sizes = [capacity * len(group) for group in GROUPS]
    pieces = [size * LANES for size in UNITS]
    state = {}
    turn = [hidden]

    def next_turn(value):
        return after_all(value, turn[-1])

    def gather(g):
        rows, squares = call(
            rows_kernel,
            [((sizes[g], width), BF16), ((PAD, LANES), BF16)],
            [VMEM] * (1 + len(GROUPS[g])),
            (),
            0,
            4 * sizes[g] * width,
        )(next_turn(moe_row), *[arrived[k] for k in GROUPS[g]])
        state["rows", g], state["squares", g] = rows, squares
        turn.append(rows)

    def up(g, *parts_of):
        size = sizes[g]
        outs, inputs, jobs = [], [], []
        for c, home in parts_of:
            extra = c == 0 and not home
            outs.append(((size + PAD * extra, 4 * pieces[c]), F32 if home else BF16))
            inputs += [gates[c], ups[c]]
            jobs.append((home, extra))
        made = call(
            functools.partial(up_kernel, jobs),
            outs,
            [SMEM] + [VMEM] * (2 + len(inputs)),
            (),
            8 * size * width * sum(pieces[c] for c, _ in parts_of),
            8 * size * width,
        )(part, next_turn(state["rows", g]), state["squares", g], *inputs)
        made = [made] if len(outs) == 1 else list(made)
        turn.append(made[0])
        for (c, home), sums in zip(parts_of, made):
            if home:
                state["home", g, c] = sums
            else:
                state["came", g, c] = lax.ppermute(sums, "head", flip(parts, 1))

    def add(g, c):
        size, piece, extra = sizes[g], pieces[c], c == 0
        cross, state["stay", g, c], *lines = call(
            functools.partial(add_kernel, extra),
            [((size + PAD * extra, 2 * piece), BF16), ((size, 2 * piece), F32)]
            + [((PAD, LANES), F32)] * extra,
            [VMEM] * 3,
            (),
            0,
            32 * size * piece,
        )(next_turn(state["home", g, c]), state["came", g, c], state["squares", g])
        if extra:
            state["lines", g] = lines[0]
        state["seen", g, c] = lax.ppermute(cross, "head", flip(parts, 2))
        turn.append(cross)

    def act(g, c):
        size, piece, extra = sizes[g], pieces[c], c == 0
        made = call(
            functools.partial(act_kernel, float(width * parts), extra),
            [((size, piece), BF16)] + [((size, 8), F32)] * extra,
            [VMEM] * 3,
            (),
            0,
            10 * size * piece,
        )(
            next_turn(state["stay", g, c]),
            state["seen", g, c],
            state["lines" if extra else "scale", g],
        )
        if extra:
            made, state["scale", g] = made
        across = lax.ppermute(made, "head", flip(parts, 2))
        beside = lax.ppermute(made, "head", flip(parts, 1))
        state["acts", g, c] = [made, across, beside]
        turn.append(made)

    def down(g, c):
        size, piece, last = sizes[g], pieces[c], c == chunks[-1]
        made, across, beside = state["acts", g, c]
        diagonal = lax.ppermute(across, "head", flip(parts, 1))
        acc = state.get(("acc", g))
        out = call(
            functools.partial(down_kernel, c == 0),
            [((capacity, width), BF16)] * len(GROUPS[g]) if last else [((size, width), F32)],
            [SMEM] + [VMEM] * (5 + (c > 0)),
            (),
            8 * size * width * piece,
            8 * size * width,
        )(part, next_turn(made), across, beside, diagonal, *([acc] if c else []), downs[c])
        state["acc", g] = out
        turn.append(out[0] if last else out)
        if last:
            for k, block in zip(GROUPS[g], out):
                returned[k] = exchange(block, k)

    def late_fetch(n):
        turn.append(fetch(FETCHES[n], turn[-1]))

    returned = {}
    for job, *where in PLAN:
        {"gather": gather, "up": up, "add": add, "act": act, "down": down, "fetch": late_fetch}[job](*where)
    stats = lax.psum(next_turn(stats), "head")
    return call(
        functools.partial(combine_kernel, float(width * parts)),
        [((length, width), BF16)],
        [SMEM] + [VMEM] * (3 + spots),
        [pltpu.VMEM((count, length), jnp.int32), pltpu.VMEM((count, length), F32)],
        4 * length * count * capacity * width,
        8 * length * width,
    )(spot, hidden, stats, pinned(routes_t), *[returned[k] for k in range(spots)])


PLAN = (
    ("fetch", 0),
    ("gather", 0),
    ("up", 0, (0, False)),
    ("up", 0, (0, True), (1, False)),
    ("add", 0, 0),
    ("up", 0, (1, True), (2, False)),
    ("add", 0, 1),
    ("fetch", 1),
    ("act", 0, 0),
    ("up", 0, (2, True)),
    ("add", 0, 2),
    ("act", 0, 1),
    ("act", 0, 2),
    ("down", 0, 0),
    ("down", 0, 1),
    ("down", 0, 2),
)


def local(*args):
    queries, log_decay, router, w_gate = args[0], args[3], args[8], args[10]
    spots, parts = lax.axis_size("seq"), lax.axis_size("head")
    heads = log_decay.shape[1]
    fits = (
        router.shape[1] == spots == sum(map(len, GROUPS))
        and parts == 4
        and heads % 2 == 0
        and queries.shape == (LANES, heads * LANES)
        and w_gate.shape[1] == sum(UNITS) * parts * LANES
    )
    return local_fast(*args) if fits else local_general(*args)


def solution(mesh):
    return jax.shard_map(
        local,
        mesh=mesh,
        in_specs=(
            P("seq", "head"),
            P("seq", "head"),
            P("seq", "head"),
            P("seq", "head"),
            P("seq", "head"),
            P("head"),
            P("seq", "head"),
            P("head"),
            P("head", None),
            P("seq", None),
            P("head", "seq"),
            P("head", "seq"),
            P("seq", "head"),
        ),
        out_specs=P("seq", "head"),
        check_vma=False,
    )
```

```python
import functools

import jax
import jax.numpy as jnp
from jax import lax
from jax.experimental import pallas as pl
from jax.experimental.pallas import tpu as pltpu
from jax.sharding import PartitionSpec as P


def prefix_2(value, axis, join, neutral):
    count, mine = (lax.axis_size(axis), lax.axis_index(axis))
    pieces = jax.tree.map(lambda part: lax.all_gather(part, axis), value)
    subtotal = jax.tree.map(
        lambda part, zero: jnp.full_like(part, 0) + jnp.asarray(zero, part.dtype), value, neutral
    )

    def lap(position, subtotal):
        longer = join(subtotal, jax.tree.map(lambda part: part[position], pieces))
        return jax.tree.map(lambda new, old: jnp.where(position < mine, new, old), longer, subtotal)

    return lax.fori_loop(0, count - 1, lap, subtotal)


def block_terms(query_act, key_act, value_all, decay_log):
    length = query_act.shape[0]
    cumulative = jnp.cumsum(decay_log, axis=0)
    row_index = lax.broadcasted_iota(jnp.int32, (length, length), 0)
    col_index = lax.broadcasted_iota(jnp.int32, (length, length), 1)
    causal = (row_index >= col_index)[None, :, :]
    by_head = jnp.transpose(cumulative)
    spread = by_head[:, :, None] - by_head[:, None, :]
    weight = jnp.where(causal, jnp.exp(jnp.where(causal, spread, 0.0)), 0.0)
    scores = (
        jnp.einsum("ihe,jhe->hij", query_act, key_act, precision=lax.Precision.HIGHEST) * weight
    )
    inner_part = jnp.einsum("hij,jhe->ihe", scores, value_all, precision=lax.Precision.HIGHEST)
    tail_decay = jnp.exp(cumulative[-1][None, :] - cumulative)
    local_state = jnp.einsum(
        "jhe,jhf->hef", key_act * tail_decay[:, :, None], value_all, precision=lax.Precision.HIGHEST
    )
    return (cumulative, inner_part, local_state, jnp.exp(cumulative[-1]))


def attention_out(inner_part, cumulative, carry_state, query_act):
    earlier = jnp.einsum("ihe,hef->ihf", query_act, carry_state, precision=lax.Precision.HIGHEST)
    return inner_part + jnp.exp(cumulative)[:, :, None] * earlier


def finish(attn, attn_gain, out_gate, residual):
    mean_sq = jnp.mean(attn * attn, axis=-1, keepdims=True)
    normed_heads = attn * lax.rsqrt(mean_sq + 1e-06)
    flat = normed_heads.reshape(attn.shape[0], attn.shape[1] * attn.shape[2])
    gated = flat * attn_gain.astype(jnp.float32) * jax.nn.sigmoid(out_gate.astype(jnp.float32))
    return (residual.astype(jnp.float32) + gated).astype(jnp.bfloat16)


def gate_weights(logits, routes):
    expert_ids = lax.broadcasted_iota(jnp.int32, (1, 1, logits.shape[1]), 2)
    onehot = routes[:, :, None] == expert_ids
    picked = jnp.sum(jnp.where(onehot, logits[:, None, :], 0.0), axis=-1)
    return jax.nn.sigmoid(picked - picked[:, ::-1])


def slot_table(routes, expert_count, capacity):
    flat_ids = routes.reshape(-1)
    expert_ids = lax.broadcasted_iota(jnp.int32, (1, expert_count), 1)
    onehot = (flat_ids[:, None] == expert_ids).astype(jnp.int32)
    ranking = jnp.cumsum(onehot, axis=0) - onehot
    own_rank = jnp.sum(ranking * onehot, axis=1)
    slot_ids = flat_ids * capacity + own_rank
    slot_range = lax.broadcasted_iota(jnp.int32, (1, expert_count * capacity), 1)
    return (slot_ids[:, None] == slot_range).astype(jnp.float32)


def build_sends(tok_rows, slot_bf16, expert_count, capacity, owner_count):
    doubled = jnp.repeat(tok_rows, 2, axis=0)
    packed = jnp.einsum("as,ad->sd", slot_bf16, doubled, preferred_element_type=jnp.float32).astype(
        jnp.bfloat16
    )
    width = tok_rows.shape[1]
    fanned = jnp.broadcast_to(
        packed.reshape(expert_count, 1, capacity, width),
        (expert_count, owner_count, capacity, width),
    )
    return fanned.reshape(expert_count * owner_count, capacity, width)


def local_general(
    queries,
    keys,
    values,
    log_decay,
    out_gate,
    attn_gain,
    residual,
    moe_gain,
    router,
    routes,
    w_gate,
    w_up,
    w_down,
):
    tok_count = queries.shape[0]
    heads_here = log_decay.shape[1]
    head_size = queries.shape[1] // heads_here
    query_act = jax.nn.silu(queries.astype(jnp.float32)).reshape(tok_count, heads_here, head_size)
    key_act = jax.nn.silu(keys.astype(jnp.float32)).reshape(tok_count, heads_here, head_size)
    value_all = values.astype(jnp.float32).reshape(tok_count, heads_here, head_size)
    cumulative, inner_part, local_state, block_decay = block_terms(
        query_act, key_act, value_all, log_decay
    )

    def combine(earlier, later):
        return (earlier[0] * later[0], later[0][:, None, None] * earlier[1] + later[1])

    identity = (jnp.ones_like(block_decay), jnp.zeros_like(local_state))
    prefix = prefix_2((block_decay, local_state), "seq", combine, identity)
    attn = attention_out(inner_part, cumulative, prefix[1], query_act)
    hidden = finish(attn, attn_gain, out_gate, residual)
    part_width = hidden.shape[1]
    full_width = part_width * lax.axis_size("head")
    wide = hidden.astype(jnp.float32)
    squares = lax.psum(jnp.sum(wide * wide, axis=1), "head")
    scale = lax.rsqrt(squares / full_width + 1e-06)
    normed = (wide * scale[:, None] * moe_gain.astype(jnp.float32)).astype(jnp.bfloat16)
    logits = lax.psum(jnp.dot(normed, router, preferred_element_type=jnp.float32), "head")
    weights = gate_weights(logits, routes)
    expert_count = router.shape[1]
    owner_count = lax.axis_size("seq") // expert_count
    capacity = 2 * tok_count // expert_count + max(1, tok_count // 32)
    table = slot_table(routes, expert_count, capacity)
    outgoing = build_sends(normed, table.astype(jnp.bfloat16), expert_count, capacity, owner_count)
    arrived = lax.all_to_all(outgoing, "seq", split_axis=0, concat_axis=0, tiled=True)
    sources, items, width = arrived.shape
    flat_rows = arrived.reshape(sources * items, width)
    gate_part = jnp.dot(flat_rows, w_gate, preferred_element_type=jnp.float32)
    up_part = jnp.dot(flat_rows, w_up, preferred_element_type=jnp.float32)
    gate = lax.psum_scatter(gate_part, "head", scatter_dimension=1, tiled=True)
    upward = lax.psum_scatter(up_part, "head", scatter_dimension=1, tiled=True)
    act = (jax.nn.silu(gate) * upward).astype(jnp.bfloat16)
    act = lax.all_gather(act, "head", axis=1, tiled=True)
    result = jnp.dot(act, w_down, preferred_element_type=jnp.float32).astype(jnp.bfloat16)
    shares = result.reshape(sources, items, width)
    returned = lax.all_to_all(shares, "seq", split_axis=0, concat_axis=0, tiled=True)
    summed = (
        returned.astype(jnp.float32)
        .reshape(expert_count, owner_count, capacity, part_width)
        .sum(axis=1)
    )
    summed = summed.reshape(expert_count * capacity, part_width)
    per_token = (
        (table * weights.reshape(-1)[:, None])
        .reshape(tok_count, 2, expert_count * capacity)
        .sum(axis=1)
    )
    moe = jnp.dot(per_token, summed, precision=lax.Precision.HIGHEST)
    return (hidden.astype(jnp.float32) + moe).astype(jnp.bfloat16)


F32, BF16 = jnp.float32, jnp.bfloat16
LANES = 128
PAD = 16
NT = (((1,), (1,)), ((), ()))
TN = (((0,), (0,)), ((), ()))


def mm(a, b, dims=(((1,), (0,)), ((), ()))):
    return lax.dot_general(a, b, dims, preferred_element_type=F32)


def exact(a, b, dims=(((1,), (0,)), ((), ()))):
    return lax.dot_general(
        a, b, dims, preferred_element_type=F32, precision=lax.Precision.HIGHEST
    )


def split2(a):
    high = a.astype(BF16)
    return high, (a - high.astype(F32)).astype(BF16)


def silu(a):
    return a / (1.0 + jnp.exp(-a))


def decay_rows(decay_ref):
    heads, length = decay_ref.shape
    row = lax.broadcasted_iota(jnp.int32, (length, length), 0)
    col = lax.broadcasted_iota(jnp.int32, (length, length), 1)
    return exact(decay_ref[...], (row <= col).astype(F32)), row, col


def spread(values):
    high, low = split2(jnp.broadcast_to(values, (values.shape[0], LANES)))
    rest = PAD - 2 * values.shape[0]
    return jnp.concatenate([high, low, jnp.zeros((rest, LANES), BF16)], axis=0)


def state_kernel(place_ref, keys_ref, values_ref, decay_ref, sent_ref, kept_ref, own_ref, all_ref, dec_ref):
    heads, length = decay_ref.shape
    half = heads // 2
    cum, _, _ = decay_rows(decay_ref)
    total = cum[:, length - 1 :]
    tail = jnp.transpose(jnp.exp(total - cum))
    whole = jnp.exp(total)
    for h in range(heads):
        lanes = pl.ds(h * LANES, LANES)
        act = silu(keys_ref[:, lanes].astype(F32)) * tail[:, h : h + 1]
        high, low = split2(act)
        value = values_ref[:, lanes]
        all_ref[h] = mm(high, value, TN) + mm(low, value, TN)
    dec_ref[0] = jnp.broadcast_to(whole[:half], (half, LANES))
    dec_ref[1] = jnp.broadcast_to(whole[half:], (half, LANES))
    mine = place_ref[0] % 2
    for i in range(half):
        sent_ref[pl.ds(i * LANES, LANES), :] = all_ref[(1 - mine) * half + i].astype(BF16)
        kept_ref[i] = all_ref[mine * half + i]
    sent_ref[pl.ds(half * LANES, PAD), :] = spread(dec_ref[1 - mine])
    own_ref[...] = dec_ref[mine]


def inner_kernel(
    queries_ref, keys_ref, values_ref, decay_ref, inner_ref, high_ref, low_ref
):
    heads, length = decay_ref.shape
    cum, row, col = decay_rows(decay_ref)
    columns = jnp.transpose(cum)
    grown = jnp.exp(columns)
    causal = row >= col
    for h in range(heads):
        lanes = pl.ds(h * LANES, LANES)
        query = silu(queries_ref[:, lanes].astype(F32))
        high_ref[:, lanes], low_ref[:, lanes] = split2(query * grown[:, h : h + 1])
        q_high, q_low = split2(query)
        k_high, k_low = split2(silu(keys_ref[:, lanes].astype(F32)))
        gap = jnp.where(causal, columns[:, h : h + 1] - cum[h : h + 1, :], 0.0)
        weight = jnp.where(causal, jnp.exp(gap), 0.0)
        scores = (mm(q_high, k_high, NT) + (mm(q_high, k_low, NT) + mm(q_low, k_high, NT))) * weight
        high, low = split2(scores)
        value = values_ref[:, lanes]
        inner_ref[:, lanes] = mm(high, value) + mm(low, value)


def gate_kernel(gain_ref, gate_ref, out_ref):
    gate = 1.0 / (1.0 + jnp.exp(-gate_ref[...].astype(F32)))
    out_ref[...] = gate * gain_ref[...].astype(F32)


def expert_table(routes_ref, count):
    length = routes_ref.shape[1]
    ids = lax.broadcasted_iota(jnp.int32, (count, length), 0)
    first = routes_ref[0:1, :] == ids
    second = routes_ref[1:2, :] == ids
    named = jnp.where(first | second, 1.0, 0.0)
    row = lax.broadcasted_iota(jnp.int32, (length, length), 0)
    col = lax.broadcasted_iota(jnp.int32, (length, length), 1)
    rank = mm(named.astype(BF16), jnp.where(row < col, 1.0, 0.0).astype(BF16))
    return first, second, jnp.where(named > 0.0, rank.astype(jnp.int32), -1)


def hidden_kernel(
    place_ref, high_ref, low_ref, inner_ref, own_ref, other_ref, gate_ref,
    residual_ref, moe_gain_ref, router_ref, routes_ref, hidden_ref, stats_ref, *rest,
):
    packed_refs, rank_ref = rest[:-1], rest[-1]
    half = own_ref.shape[0]
    heads, length = 2 * half, inner_ref.shape[0]
    count, slots = len(packed_refs), packed_refs[0].shape[0]
    first_half = place_ref[0] % 2 == 0
    squares = jnp.zeros((length, LANES), F32)
    logits = jnp.zeros((count, length), F32)
    for h in range(heads):
        lanes = pl.ds(h * LANES, LANES)
        mine, other = own_ref[h % half], other_ref[pl.ds((h % half) * LANES, LANES), :]
        carry = jnp.where(first_half == (h < half), mine, other)
        attn = inner_ref[:, lanes] + (mm(high_ref[:, lanes], carry) + mm(low_ref[:, lanes], carry))
        mean_sq = jnp.mean(attn * attn, axis=1, keepdims=True)
        gated = attn * lax.rsqrt(mean_sq + 1e-06) * gate_ref[:, lanes]
        hidden = (residual_ref[:, lanes].astype(F32) + gated).astype(BF16)
        hidden_ref[:, lanes] = hidden
        wide = hidden.astype(F32)
        squares = squares + wide * wide
        scaled = (wide * moe_gain_ref[:, lanes].astype(F32)).astype(BF16)
        logits = logits + mm(router_ref[:, lanes], scaled, NT)
    stats_ref[0:count, :] = logits
    stats_ref[count:, :] = exact(jnp.ones((8, LANES), F32), squares, NT)
    _, _, rank = expert_table(routes_ref, count)
    rank_ref[...] = rank
    rows = hidden_ref[...]
    slot = lax.broadcasted_iota(jnp.int32, (slots, length), 0)
    for k, packed_ref in enumerate(packed_refs):
        pick = jnp.where(rank_ref[pl.ds(place_ref[0] ^ k, 1), :] == slot, 1.0, 0.0).astype(BF16)
        packed_ref[...] = mm(pick, rows).astype(BF16)


def rows_kernel(moe_gain_ref, *rest):
    arrived_refs, (rows_ref, squares_ref) = rest[:-2], rest[-2:]
    capacity, width = arrived_refs[0].shape
    total = len(arrived_refs) * capacity
    groups = pl.cdiv(total, LANES)
    sums = []
    for s, arrived_ref in enumerate(arrived_refs):
        wide = arrived_ref[...].astype(F32)
        rows_ref[pl.ds(s * capacity, capacity), :] = (wide * moe_gain_ref[...].astype(F32)).astype(BF16)
        square = wide * wide
        part = square[:, :LANES]
        for k in range(1, width // LANES):
            part = part + square[:, k * LANES : (k + 1) * LANES]
        sums.append(part)
    sums = jnp.concatenate(sums + [jnp.zeros((groups * LANES - total, LANES), F32)], axis=0)
    ones = jnp.ones((8, LANES), F32)
    lines = [exact(ones, sums[g * LANES : (g + 1) * LANES], NT)[0:1] for g in range(groups)]
    high, low = split2(jnp.concatenate(lines, axis=0))
    squares_ref[...] = jnp.concatenate(
        [high, low, jnp.zeros((PAD - 2 * groups, LANES), BF16)], axis=0
    )


def fetch_kernel(jobs, gate_ref, up_ref, down_ref, *rest):
    targets, sems = rest[:-1], rest[-1]
    copies = []
    for n, (which, start, size) in enumerate(jobs):
        if which == 2:
            source = down_ref.at[pl.ds(start, size), :]
        else:
            source = (gate_ref, up_ref)[which].at[:, pl.ds(start, size)]
        copies.append(pltpu.make_async_copy(source, targets[n], sems.at[n]))
    for copy in copies:
        copy.start()
    for copy in copies:
        copy.wait()


def chosen(place_ref, other_y, other_core):
    core, y = place_ref[0] % 2, place_ref[0] // 2
    return (1 - y if other_y else y) * 2 + (1 - core if other_core else core)


def up_part(home, place_ref, rows_ref, gate_ref, up_ref, out_ref):
    piece = gate_ref.shape[1] // 4
    for k in range(2):
        start = pl.multiple_of(chosen(place_ref, k == 0, not home) * piece, LANES)
        for i, weights in enumerate((gate_ref, up_ref)):
            lanes = pl.ds((2 * k + i) * piece, piece)
            sums = mm(rows_ref[...], weights[:, pl.ds(start, piece)])
            out_ref[pl.ds(0, rows_ref.shape[0]), lanes] = sums.astype(out_ref.dtype)


def up_kernel(jobs, place_ref, rows_ref, squares_ref, *refs):
    total = rows_ref.shape[0]
    for n, (home, extra) in enumerate(jobs):
        out_ref = refs[2 * len(jobs) + n]
        if extra:
            left = out_ref.shape[1] - LANES
            out_ref[pl.ds(total, PAD), pl.ds(0, LANES)] = squares_ref[...]
            out_ref[pl.ds(total, PAD), pl.ds(LANES, left)] = jnp.zeros((PAD, left), BF16)
        up_part(home, place_ref, rows_ref, refs[2 * n], refs[2 * n + 1], out_ref)


def add_kernel(extra, home_ref, came_ref, squares_ref, cross_ref, stay_ref, *more):
    total, width = stay_ref.shape
    for k in range(2):
        lanes = pl.ds(k * width, width)
        sums = home_ref[:, lanes] + came_ref[pl.ds(0, total), lanes].astype(F32)
        if k:
            stay_ref[...] = sums
        else:
            cross_ref[pl.ds(0, total), :] = sums.astype(BF16)
    if extra:
        groups = pl.cdiv(total, LANES)
        seen = came_ref[pl.ds(total, PAD), pl.ds(0, LANES)].astype(F32) + squares_ref[...].astype(F32)
        line_sum = seen[:groups] + seen[groups : 2 * groups]
        more[0][...] = jnp.concatenate([line_sum, jnp.zeros((PAD - groups, LANES), F32)], axis=0)
        high, low = split2(line_sum)
        lines = jnp.concatenate([high, low, jnp.zeros((PAD - 2 * groups, LANES), BF16)], axis=0)
        cross_ref[pl.ds(total, PAD), pl.ds(0, LANES)] = lines
        cross_ref[pl.ds(total, PAD), pl.ds(LANES, width - LANES)] = jnp.zeros((PAD, width - LANES), BF16)


def act_kernel(full_width, extra, stay_ref, seen_ref, scale_ref, act_ref, *more):
    total, piece = act_ref.shape
    if extra:
        groups = pl.cdiv(total, LANES)
        lines = seen_ref[pl.ds(total, PAD), pl.ds(0, LANES)].astype(F32)
        line_sum = scale_ref[0:groups, :] + lines[:groups] + lines[groups : 2 * groups]
        factor = lax.rsqrt(line_sum / full_width + 1e-06)
        columns = [jnp.transpose(jnp.broadcast_to(factor[g : g + 1], (8, LANES))) for g in range(groups)]
        scale = jnp.concatenate(columns, axis=0)[:total]
        more[0][...] = scale
        scale = scale[:, 0:1]
    else:
        scale = scale_ref[:, 0:1]
    joined = stay_ref[...] + seen_ref[pl.ds(0, total), :].astype(F32)
    act_ref[...] = (silu(scale * joined[:, :piece]) * (scale * joined[:, piece:])).astype(BF16)


def down_kernel(start, place_ref, *rest):
    acts, rest = rest[:4], rest[4:]
    total, (down_ref, *out_refs) = (None, rest) if start else (rest[0][...], rest[1:])
    piece = acts[0].shape[1]
    for n in range(4):
        row = pl.multiple_of(chosen(place_ref, n % 2 == 1, n >= 2) * piece, LANES)
        term = mm(acts[n][...], down_ref[pl.ds(row, piece), :])
        total = term if total is None else total + term
    if out_refs[0].dtype == F32:
        out_refs[0][...] = total
    else:
        for s, out_ref in enumerate(out_refs):
            capacity = out_ref.shape[0]
            out_ref[...] = total[s * capacity : (s + 1) * capacity].astype(BF16)


def weights_kernel(full_width, place_ref, stats_ref, routes_ref, high_ref, low_ref, rank_ref, weight_ref):
    count, slots, length = high_ref.shape
    first, second, rank_ref[...] = expert_table(routes_ref, count)
    scale = lax.rsqrt(stats_ref[count : count + 1, :] / full_width + 1e-06)
    logits = stats_ref[0:count, :] * scale
    gap = jnp.sum(jnp.where(first, logits, 0.0), axis=0, keepdims=True) - jnp.sum(
        jnp.where(second, logits, 0.0), axis=0, keepdims=True
    )
    weight_ref[...] = jnp.where(first, 1.0 / (1.0 + jnp.exp(-gap)), 1.0 / (1.0 + jnp.exp(gap)))
    slot = lax.broadcasted_iota(jnp.int32, (slots, length), 0)
    for k in range(count):
        line = pl.ds(place_ref[0] ^ k, 1)
        pick = jnp.where(rank_ref[line, :] == slot, weight_ref[line, :], 0.0)
        high_ref[k], low_ref[k] = split2(pick)


def combine_kernel(order, high_ref, low_ref, hidden_ref, *rest):
    returned_refs, out_ref = rest[:-1], rest[-1]
    total = hidden_ref[...].astype(F32)
    for k, returned_ref in zip(order, returned_refs):
        rows = returned_ref[...]
        total = total + mm(high_ref[k], rows, TN) + mm(low_ref[k], rows, TN)
    out_ref[...] = total.astype(BF16)


LIGHT = 1
VMEM = pl.BlockSpec(memory_space=pltpu.VMEM)
SMEM = pl.BlockSpec(memory_space=pltpu.SMEM)
ANY = pl.BlockSpec(memory_space=pl.ANY)


def call(kernel, outs, specs, scratch=(), flops=0, moved=0, room=6):
    shapes = [jax.ShapeDtypeStruct(*out) for out in outs]
    single = len(shapes) == 1
    return pl.pallas_call(
        kernel,
        out_shape=shapes[0] if single else shapes,
        in_specs=specs,
        out_specs=VMEM if single else [VMEM] * len(shapes),
        scratch_shapes=list(scratch),
        cost_estimate=pl.CostEstimate(flops=flops // LIGHT, bytes_accessed=moved // LIGHT, transcendentals=0),
        compiler_params=pltpu.CompilerParams(vmem_limit_bytes=room << 20),
    )


def pinned(array):
    return pltpu.with_memory_space_constraint(array, pltpu.HBM)


def after_all(value, *others):
    return lax.optimization_barrier((value,) + others)[0]


def flip(count, bit):
    return [(i, i ^ bit) for i in range(count)]


def shift(count, step):
    return [(i, i + step) for i in range(count - step)]


def unpack(message, half):
    state = message[: half * LANES].astype(F32).reshape(half, LANES, LANES)
    lines = message[half * LANES :].astype(F32)
    return state, (lines[:half] + lines[half : 2 * half])[:, None, :]


def pack(state, decay):
    half = state.shape[0]
    return jnp.concatenate([state.astype(BF16).reshape(half * LANES, LANES), spread(decay[:, 0, :])])


UNITS = (2, 4, 3)
FETCHES = tuple(tuple((name, c) for name in names for c in range(len(UNITS))) for names in ("gu", "d"))
GROUPS = ((0, 1, 2, 3, 4, 5, 6, 7),)


def local_fast(
    queries, keys, values, log_decay, out_gate, attn_gain, residual, moe_gain, router, routes,
    w_gate, w_up, w_down,
):
    length, width = queries.shape
    heads = log_decay.shape[1]
    half = heads // 2
    spots, parts = lax.axis_size("seq"), lax.axis_size("head")
    place, part = lax.axis_index("seq"), lax.axis_index("head")
    count = router.shape[1]
    capacity = 2 * length // count + max(1, length // 32)
    hidden_units = w_gate.shape[1]
    decay_t, routes_t, router_t = log_decay.T, routes.T, router.T
    spot = place.astype(jnp.int32).reshape(1)

    head_flops = 2 * length * LANES * LANES * heads
    sent, kept, own_decay = call(
        state_kernel,
        [((half * LANES + PAD, LANES), BF16), ((half, LANES, LANES), F32), ((half, LANES), F32)],
        [SMEM, VMEM, VMEM, VMEM],
        [pltpu.VMEM((heads, LANES, LANES), F32), pltpu.VMEM((2, half, LANES), F32)],
        2 * head_flops,
        6 * length * width,
    )(spot, pinned(keys), pinned(values), pinned(decay_t))
    own_decay = own_decay[:, None, :]
    inner, query_high, query_low = call(
        inner_kernel,
        [((length, width), F32), ((length, width), BF16), ((length, width), BF16)],
        [VMEM] * 4,
        (),
        5 * head_flops,
        16 * length * width,
    )(pinned(queries), pinned(keys), pinned(values), pinned(decay_t))

    gates, ups, downs = {}, {}, {}

    def fetch(names, token):
        jobs, shapes = [], []
        for name, c in names:
            span = spans[c]
            size = span.stop - span.start
            jobs.append(("gud".index(name), span.start, size))
            shapes.append(pltpu.VMEM((size, width) if name == "d" else (width, size), BF16))
        moved = pl.pallas_call(
            functools.partial(fetch_kernel, jobs),
            out_shape=shapes,
            in_specs=[ANY] * 3,
            out_specs=[VMEM] * len(jobs),
            scratch_shapes=[pltpu.SemaphoreType.DMA((len(jobs),))],
            cost_estimate=pl.CostEstimate(flops=0, bytes_accessed=1 << 20, transcendentals=0),
            compiler_params=pltpu.CompilerParams(vmem_limit_bytes=2 << 20),
        )(*[pinned(after_all(w, token)) for w in (w_gate, w_up, w_down)])
        for (name, c), array in zip(names, moved):
            {"g": gates, "u": ups, "d": downs}[name][c] = array
        return moved[0]

    even = place % 2 == 0
    part = part.astype(jnp.int32).reshape(1)
    chunks = range(len(UNITS))
    ends = [sum(UNITS[: c + 1]) * parts * LANES for c in chunks]
    spans = [slice(ends[c - 1] if c else 0, ends[c]) for c in chunks]

    theirs, their_decay = unpack(lax.ppermute(sent, "seq", flip(spots, 1)), half)
    kept = after_all(kept, inner)
    block = jnp.where(even, their_decay, 1.0) * kept + jnp.where(even, 1.0, own_decay) * theirs
    block_decay = own_decay * their_decay
    carry, between = jnp.zeros_like(block), jnp.ones_like(block_decay)
    step = 1
    while 2 * step < spots:
        window = pack(block + block_decay * carry, block_decay * between)
        if step == 1:
            gain_row = after_all(attn_gain, window).reshape(1, width)
            moe_row = after_all(moe_gain, window).reshape(1, width)
            gate = call(gate_kernel, [((length, width), F32)], [VMEM] * 2, (), 0, 6 * length * width)(
                gain_row, pinned(out_gate)
            )
        if step == 2:
            window = after_all(window, gate, moe_row)
        got, got_decay = unpack(lax.ppermute(window, "seq", shift(spots, 2 * step)), half)
        carry, between = carry + between * got, between * got_decay
        step *= 2
    after = jnp.where(even, own_decay, their_decay) * carry + jnp.where(even, kept, theirs)
    mine = jnp.where(even, carry, after).astype(BF16)
    other = jnp.where(even, after, carry).astype(BF16).reshape(half * LANES, LANES)
    other = lax.ppermute(other, "seq", flip(spots, 1))

    hidden, stats, *packed = call(
        hidden_kernel,
        [((length, width), BF16), ((count + 8, length), F32)] + [((capacity, width), BF16)] * spots,
        [SMEM] + [VMEM] * 10,
        [pltpu.VMEM((count, length), jnp.int32)],
        3 * head_flops,
        16 * length * width,
    )(
        spot, query_high, query_low, inner, mine, other, gate, pinned(residual),
        moe_row, pinned(router_t), pinned(routes_t),
    )
    def exchange(block, k):
        return lax.ppermute(block, "seq", flip(spots, k)) if k else block

    arrived = [exchange(block, k) for k, block in enumerate(packed)]
    sizes = [capacity * len(group) for group in GROUPS]
    pieces = [size * LANES for size in UNITS]
    state = {}
    turn = [hidden]

    def next_turn(value):
        return after_all(value, turn[-1])

    def gather(g):
        rows, squares = call(
            rows_kernel,
            [((sizes[g], width), BF16), ((PAD, LANES), BF16)],
            [VMEM] * (1 + len(GROUPS[g])),
            (),
            0,
            4 * sizes[g] * width,
        )(next_turn(moe_row), *[arrived[k] for k in GROUPS[g]])
        state["rows", g], state["squares", g] = rows, squares
        turn.append(rows)

    def up(g, *parts_of):
        size = sizes[g]
        outs, inputs, jobs = [], [], []
        for c, home in parts_of:
            extra = c == 0 and not home
            outs.append(((size + PAD * extra, 4 * pieces[c]), F32 if home else BF16))
            inputs += [gates[c], ups[c]]
            jobs.append((home, extra))
        made = call(
            functools.partial(up_kernel, jobs),
            outs,
            [SMEM] + [VMEM] * (2 + len(inputs)),
            (),
            8 * size * width * sum(pieces[c] for c, _ in parts_of),
            8 * size * width,
        )(part, next_turn(state["rows", g]), state["squares", g], *inputs)
        made = [made] if len(outs) == 1 else list(made)
        turn.append(made[0])
        for (c, home), sums in zip(parts_of, made):
            if home:
                state["home", g, c] = sums
            else:
                state["came", g, c] = lax.ppermute(sums, "head", flip(parts, 1))

    def add(g, c):
        size, piece, extra = sizes[g], pieces[c], c == 0
        cross, state["stay", g, c], *lines = call(
            functools.partial(add_kernel, extra),
            [((size + PAD * extra, 2 * piece), BF16), ((size, 2 * piece), F32)]
            + [((PAD, LANES), F32)] * extra,
            [VMEM] * 3,
            (),
            0,
            32 * size * piece,
        )(next_turn(state["home", g, c]), state["came", g, c], state["squares", g])
        if extra:
            state["lines", g] = lines[0]
        state["seen", g, c] = lax.ppermute(cross, "head", flip(parts, 2))
        turn.append(cross)

    def act(g, c):
        size, piece, extra = sizes[g], pieces[c], c == 0
        made = call(
            functools.partial(act_kernel, float(width * parts), extra),
            [((size, piece), BF16)] + [((size, 8), F32)] * extra,
            [VMEM] * 3,
            (),
            0,
            10 * size * piece,
        )(
            next_turn(state["stay", g, c]),
            state["seen", g, c],
            state["lines" if extra else "scale", g],
        )
        if extra:
            made, state["scale", g] = made
        across = lax.ppermute(made, "head", flip(parts, 2))
        beside = lax.ppermute(made, "head", flip(parts, 1))
        state["acts", g, c] = [made, across, beside]
        turn.append(made)

    def down(g, c):
        size, piece, last = sizes[g], pieces[c], c == chunks[-1]
        made, across, beside = state["acts", g, c]
        diagonal = lax.ppermute(across, "head", flip(parts, 1))
        acc = state.get(("acc", g))
        out = call(
            functools.partial(down_kernel, c == 0),
            [((capacity, width), BF16)] * len(GROUPS[g]) if last else [((size, width), F32)],
            [SMEM] + [VMEM] * (5 + (c > 0)),
            (),
            8 * size * width * piece,
            8 * size * width,
        )(part, next_turn(made), across, beside, diagonal, *([acc] if c else []), downs[c])
        state["acc", g] = out
        turn.append(out[0] if last else out)
        if last:
            for k, block in zip(GROUPS[g], out):
                returned[k] = exchange(block, k)

    def late_fetch(n):
        turn.append(fetch(FETCHES[n], turn[-1]))

    returned = {}
    for job, *where in PLAN:
        {"gather": gather, "up": up, "add": add, "act": act, "down": down, "fetch": late_fetch}[job](*where)
    stats = lax.psum(next_turn(stats), "head")
    high, low = call(
        functools.partial(weights_kernel, float(width * parts)),
        [((spots, capacity, length), BF16)] * 2,
        [SMEM] + [VMEM] * 2,
        [pltpu.VMEM((count, length), jnp.int32), pltpu.VMEM((count, length), F32)],
        0,
        4 * spots * capacity * length,
    )(spot, stats, pinned(routes_t))
    order = RETURNS
    return call(
        functools.partial(combine_kernel, order),
        [((length, width), BF16)],
        [VMEM] * (3 + spots),
        (),
        4 * length * count * capacity * width,
        8 * length * width,
    )(high, low, hidden, *[returned[k] for k in order])


RETURNS = (0, 1, 2, 3, 4, 5, 6, 7)

PLAN = (
    ("fetch", 0),
    ("gather", 0),
    ("up", 0, (0, False)),
    ("up", 0, (0, True), (1, False)),
    ("add", 0, 0),
    ("up", 0, (1, True), (2, False)),
    ("add", 0, 1),
    ("fetch", 1),
    ("act", 0, 0),
    ("up", 0, (2, True)),
    ("add", 0, 2),
    ("act", 0, 1),
    ("act", 0, 2),
    ("down", 0, 0),
    ("down", 0, 1),
    ("down", 0, 2),
)


def local(*args):
    queries, log_decay, router, w_gate = args[0], args[3], args[8], args[10]
    spots, parts = lax.axis_size("seq"), lax.axis_size("head")
    heads = log_decay.shape[1]
    fits = (
        router.shape[1] == spots == sum(map(len, GROUPS))
        and parts == 4
        and heads % 2 == 0
        and queries.shape == (LANES, heads * LANES)
        and w_gate.shape[1] == sum(UNITS) * parts * LANES
    )
    return local_fast(*args) if fits else local_general(*args)


def solution(mesh):
    return jax.shard_map(
        local,
        mesh=mesh,
        in_specs=(
            P("seq", "head"),
            P("seq", "head"),
            P("seq", "head"),
            P("seq", "head"),
            P("seq", "head"),
            P("head"),
            P("seq", "head"),
            P("head"),
            P("head", None),
            P("seq", None),
            P("head", "seq"),
            P("head", "seq"),
            P("seq", "head"),
        ),
        out_specs=P("seq", "head"),
        check_vma=False,
    )
```
